512 devices in a mesh: row: 32 (over z, core), col: 4 (over y), mem: 4 (over x).
Axes of the slice: x: 4, y: 4, z: 16, core: 2. Of those that a mesh axis runs over, the one named last changes fastest.
Arguments:
- adj_final: float32 [16384, 4096], P(('mem', 'row'), 'col'), parts along dimension 0, may hold values from -6 to 6
- kappa: float32 [16384, 4096], P(('mem', 'row'), 'col'), parts along dimension 0, may hold values from 0.1 to 1
- elev_early: float32 [16384, 4096], P(('mem', 'row'), 'col'), parts along dimension 0, may hold values from -6 to 6
- elev_late: float32 [16384, 4096], P(('mem', 'row'), 'col'), parts along dimension 0, may hold values from -6 to 6
- basis: bfloat16 [128, 4, 4, 1024, 256], P(('mem', 'row'), 'col'), parts along dimension 0, may hold values from -0.1875 to 0.1875
- basis_index: int32 [128, 4, 512], P(('mem', 'row'), 'col'), parts along dimension 0, may hold values from 0 to 3
- intersection_patch: int32 [128, 4, 512], P(('mem', 'row'), 'col'), parts along dimension 0, may hold values from 0 to 2047, as said below
- owner_row: int32 [16, 2048], P(('mem', 'col')), parts along dimension 0, may hold values from 0 to 2047, as said below
Outputs:
- adj_start: float32 [16384, 4096], P(('mem', 'row'), 'col'), parts along dimension 0
- coeff_grad: float32 [16, 2048, 256], P(('mem', 'col'), 'row'), parts along dimension 0
The draws below stay inside these ranges and needn't reach their ends.
There are 4 independent parts, one for each index of `mem`. The reference program is written for one: setup_inputs(seed, part) draws one part's arguments, and reference() takes and returns one part's arrays. A program takes and returns all parts, laid end to end along the dimension named above; each array names one. Nothing has to cross between parts.
Inputs may be any that keep to these rules, and one draw needn't show every extreme that they name: Each row of owner_row is a permutation of 0 to 2047; the owner of patch p in strip j is owner_row[j, p] // 64. `intersection_patch`: of the 512 entries of one tile (i, j), at most 32 name patches of any one owner r (patches p with owner_row[j, p] // 64 = r), and exactly 32 name patches of some owner.
All inputs are finite; a program needn't handle non-finite values.
Results may differ from the reference program's by a relative error of at most 0.0029.
Values sent between devices are 32-bit elements; how exact they have to be, the bound alone decides.
No kernel may reach another device: no remote copies, remote signals or barrier semaphores. Data moves between devices by JAX's collectives and lax.ppermute only.
A program may use at most 64 MiB of HBM per device.

```python
import math
import jax
import jax.numpy as jnp
from jax import lax

TR = 128
TC = 1024
BS = 32
NCOEF = 256
OV = 4
NQ = 4
PD = 64
NR = 4096
NC = 4096
NB = 128
ENTRIES = 512
CAP = 32
PATCHES = 2048
N_ROW = 32
N_COL = 4


def joint_lists(key):
    base = jax.random.fold_in(key, 7)
    perm_keys = jax.random.split(jax.random.fold_in(base, 1), N_COL)
    owner_table = jax.vmap(lambda k: jax.random.permutation(k, PATCHES))(perm_keys).astype(jnp.int32)
    inverse = jnp.argsort(owner_table, axis=1).astype(jnp.int32)
    slot_total = 2 * ENTRIES
    device_keys = jax.random.split(jax.random.fold_in(base, 2), N_ROW * N_COL)
    columns = jnp.arange(N_ROW * N_COL, dtype=jnp.int32) % N_COL

    def one_device(dkey, column):
        key_a, key_b, key_c, key_d = jax.random.split(dkey, 4)
        forced = jax.random.randint(key_a, (), 0, N_ROW).astype(jnp.int32)
        score = jax.random.randint(key_b, (slot_total,), 0, 1 << 14).astype(jnp.int32)
        owners = jnp.arange(slot_total, dtype=jnp.int32) // CAP
        ranking = jnp.where(owners == forced, 0, 1 << 28) + score * slot_total + jnp.arange(slot_total, dtype=jnp.int32)
        chosen = jnp.argsort(ranking)[:ENTRIES].astype(jnp.int32)
        shuffle = jax.random.permutation(key_c, ENTRIES).astype(jnp.int32)
        entry_owner = (chosen // CAP)[shuffle]
        within = jax.random.randint(key_d, (ENTRIES,), 0, PD).astype(jnp.int32)
        return inverse[column, entry_owner * PD + within]
    patches = jax.vmap(one_device)(device_keys, columns)
    return (owner_table, patches.reshape(N_ROW, N_COL, ENTRIES).astype(jnp.int32))


def draw_intersection_patch(key, part):
    return joint_lists(key)[1]


def draw_owner_row(key, part):
    return joint_lists(key)[0]


def with_ends(array, key, low, top_value):
    longest = array.shape.index(max(array.shape))
    spots = []
    for shift in (0, 1):
        where = [jax.random.randint(jax.random.fold_in(key, axis), (), 0, length) for axis, length in enumerate(array.shape)]
        where[longest] = (where[longest] + shift) % array.shape[longest]
        spots.append(tuple(where))
    return array.at[spots[0]].set(low).at[spots[1]].set(top_value)


def shard_levels(stream_key, shape, pieces, smallest, top_value):
    def one(axis_at, shards_of):
        steps = jax.random.uniform(jax.random.fold_in(jax.random.fold_in(stream_key, 6), axis_at), (shards_of,), jnp.float32, smallest / len(pieces), top_value / len(pieces))
        return jnp.repeat(jnp.exp(steps), shape[axis_at] // shards_of).reshape((-1,) + (1,) * (len(shape) - axis_at - 1))

    factor_of = one(*pieces[0])
    for cut in pieces[1:]:
        factor_of = factor_of * one(*cut)
    return factor_of


def gaussian(key, dims, spread, reach, pieces=(), kind=jnp.bfloat16):
    gain = shard_levels(key, dims, pieces, -0.22, 0.18) if pieces else 1.0
    result = jax.random.normal(key, dims, jnp.float32) * spread * gain
    return jnp.minimum(jnp.maximum(result, -reach), reach).astype(kind)


def setup_inputs(seed: int = 0, part: int = 0) -> dict:
    splits = jax.random.split(jax.random.key(seed), 9)
    part_splits = jax.random.split(jax.random.fold_in(splits[8], part), 9)
    adj_final = gaussian(part_splits[0], (NR, NC), 1.0, 6.0, ((0, 32), (1, 4)), jnp.float32)
    kappa = jnp.clip(jnp.exp(math.log(1.0) - 2.3025851 * jax.random.uniform(part_splits[1], (NR, NC), jnp.float32) ** shard_levels(part_splits[1], (NR, NC), ((0, 32), (1, 4)), -0.2, 0.2)), 0.1, 1.0)
    elev_early = gaussian(part_splits[2], (NR, NC), 1.0, 6.0, ((0, 32), (1, 4)), jnp.float32)
    elev_late = gaussian(part_splits[3], (NR, NC), 1.0, 6.0, ((0, 32), (1, 4)), jnp.float32)
    basis = gaussian(part_splits[4], (N_ROW, N_COL, NQ, BS * BS, NCOEF), (BS * BS) ** -0.5, 0.1875, ((0, 32), (1, 4)))
    basis_index = with_ends(jax.random.randint(part_splits[5], (N_ROW, N_COL, ENTRIES), 0, NQ), jax.random.fold_in(part_splits[5], 1), 0, NQ - 1).astype(jnp.int32)
    intersection_patch = draw_intersection_patch(jax.random.fold_in(jax.random.fold_in(splits[8], part), 71), part)
    owner_row = draw_owner_row(jax.random.fold_in(jax.random.fold_in(splits[8], part), 71), part)
    return dict(adj_final=adj_final, kappa=kappa, elev_early=elev_early, elev_late=elev_late, basis=basis, basis_index=basis_index, intersection_patch=intersection_patch, owner_row=owner_row)


DT = 0.2


def adjoint_step(adjoint, coef):
    padded = jnp.pad(adjoint, 1)
    centre = padded[1:-1, 1:-1]
    lap = padded[2:, 1:-1] + padded[:-2, 1:-1] + padded[1:-1, 2:] + padded[1:-1, :-2] - 4.0 * centre
    return adjoint + coef * lap


def reference(adj_final, kappa, elev_early, elev_late, basis, basis_index, intersection_patch, owner_row):
    coef_late = DT * kappa / (1.0 + elev_late * elev_late)
    coef_early = DT * kappa / (1.0 + elev_early * elev_early)
    adj_mid = adjoint_step(adj_final, coef_late)
    adj_start = adjoint_step(adj_mid, coef_early)
    grad_field = (DT * (adj_final + adj_mid)).astype(jnp.bfloat16)
    blocks = grad_field.reshape(N_ROW, TR // BS, BS, N_COL, TC // BS, BS)
    blocks = blocks.transpose(0, 3, 1, 4, 2, 5).reshape(N_ROW * N_COL, NB, BS * BS)
    tables = basis.reshape(N_ROW * N_COL, NQ, BS * BS, NCOEF)
    indices = basis_index.reshape(N_ROW * N_COL, ENTRIES).astype(jnp.int32)

    def one_tile(items):
        block_rows, table, index = items
        products = jnp.einsum('bk,qkn->qbn', block_rows.astype(jnp.float32), table.astype(jnp.float32))
        picked = products[index.reshape(NB, OV), jnp.arange(NB, dtype=jnp.int32)[:, None]]
        return picked.reshape(ENTRIES, NCOEF)

    contrib = lax.map(one_tile, (blocks, tables, indices))
    columns = jnp.arange(N_ROW * N_COL, dtype=jnp.int32) % N_COL
    patches = intersection_patch.reshape(N_ROW * N_COL, ENTRIES).astype(jnp.int32)
    targets = owner_row[columns[:, None], patches] + columns[:, None] * PATCHES
    coeff_grad = jax.ops.segment_sum(contrib.reshape(-1, NCOEF), targets.reshape(-1), num_segments=N_COL * PATCHES)
    return adj_start, coeff_grad.reshape(N_COL, PATCHES, NCOEF)
```

```python
import functools

import jax
import jax.numpy as jnp
from jax import lax
from jax.experimental import pallas as pl
from jax.experimental.pallas import tpu as pltpu
from jax.sharding import PartitionSpec as P

BS = 32
DT = 0.2
F32 = jnp.float32
BF16 = jnp.bfloat16
I32 = jnp.int32
VLIM = 24 << 20


def whole(shape):
    return jax.ShapeDtypeStruct(shape, F32)


def vmem():
    return pl.BlockSpec(memory_space=pltpu.VMEM)


def params(limit=VLIM):
    return pltpu.CompilerParams(vmem_limit_bytes=limit)


def edges_kernel(top_ref, bot_ref, left_ref, right_ref, t_ref, b_ref, l_ref, r_ref):
    t_ref[...] = top_ref[0:1, :]
    b_ref[...] = bot_ref[7:8, :]
    l_ref[...] = left_ref[...].T[0:1, :]
    r_ref[...] = right_ref[...].T[127:128, :]


def edges(a):
    rows, cols = a.shape
    return pl.pallas_call(
        edges_kernel,
        grid=(1,),
        in_specs=[
            pl.BlockSpec((8, cols), lambda i: (0, 0)),
            pl.BlockSpec((8, cols), lambda i: (rows // 8 - 1, 0)),
            pl.BlockSpec((rows, 128), lambda i: (0, 0)),
            pl.BlockSpec((rows, 128), lambda i: (0, cols // 128 - 1)),
        ],
        out_specs=[
            pl.BlockSpec((1, cols), lambda i: (0, 0)),
            pl.BlockSpec((1, cols), lambda i: (0, 0)),
            pl.BlockSpec((1, rows), lambda i: (0, 0)),
            pl.BlockSpec((1, rows), lambda i: (0, 0)),
        ],
        out_shape=[whole((1, cols)), whole((1, cols)), whole((1, rows)), whole((1, rows))],
        compiler_params=params(4 << 20),
        name="edges",
    )(a, a, a, a)


def index_kernel(core_ref, patch_ref, owner_ref, idx_ref, dest_ref, sel_ref):
    entries = patch_ref.shape[1]
    patches = owner_ref.shape[1]
    hot = lax.broadcasted_iota(I32, (patches, entries), 0) == patch_ref[...]
    hot = jnp.where(hot, 1.0, 0.0).astype(BF16)
    owner = owner_ref[...]
    row = lax.broadcasted_iota(I32, (16, patches), 0)
    parts = jnp.where(row == 0, owner >> 6, jnp.where(row == 1, owner & 63, 0))
    found = jnp.dot(parts.astype(F32).astype(BF16), hot, preferred_element_type=F32)
    high = found[0:1, :].astype(I32) ^ core_ref[0]
    low = found[1:2, :].astype(I32)
    spot = jnp.zeros_like(high)
    for bit in range(5):
        spot = spot | (((high >> bit) & 1) << (4 - bit))
    dest_ref[...] = spot * 64 + low
    nb = entries // 4
    lane = lax.broadcasted_iota(I32, (nb, entries), 1)
    block = lax.broadcasted_iota(I32, (nb, entries), 0)
    idx = jnp.broadcast_to(idx_ref[...], (nb, entries))
    for o in range(4):
        sel_ref[:, o : o + 1] = jnp.sum(
            jnp.where(lane == block * 4 + o, idx, 0), axis=1, keepdims=True
        )


def indices(core, patch, owner, idx):
    entries = patch.shape[1]
    return pl.pallas_call(
        index_kernel,
        in_specs=[pl.BlockSpec(memory_space=pltpu.SMEM), vmem(), vmem(), vmem()],
        out_specs=[vmem(), vmem()],
        out_shape=[
            jax.ShapeDtypeStruct((1, entries), I32),
            jax.ShapeDtypeStruct((entries // 4, 4), I32),
        ],
        compiler_params=params(),
        name="indices",
    )(core, patch, owner, idx)


def stencil(a_ref, kap_ref, elev_ref, n_ref, s_ref, wt, et, emit):
    rows, cols = a_ref.shape
    lane = lax.broadcasted_iota(I32, (8, cols), 1)
    sub = lax.broadcasted_iota(I32, (8, cols), 0)
    for i in range(rows // 8):
        r = 8 * i
        x = a_ref[r : r + 8, :]
        if i == 0:
            up = jnp.where(sub == 0, n_ref[...], pltpu.roll(x, 1, 0))
        else:
            up = a_ref[r - 1 : r + 7, :]
        if i == rows // 8 - 1:
            down = jnp.where(sub == 7, s_ref[...], pltpu.roll(x, 7, 0))
        else:
            down = a_ref[r + 1 : r + 9, :]
        east = jnp.where(lane == cols - 1, et[r : r + 8, 0:1], pltpu.roll(x, cols - 1, 1))
        west = jnp.where(lane == 0, wt[r : r + 8, 0:1], pltpu.roll(x, 1, 1))
        e = elev_ref[r : r + 8, :]
        coef = DT * kap_ref[r : r + 8, :] / (1.0 + e * e)
        lap = down + up + east + west - 4.0 * x
        emit(r, x, x + coef * lap)


def column(ref):
    n = ref.shape[1]
    return jnp.broadcast_to(ref[...], (128, n)).T


def hot_rows(dest, start, count):
    entries = dest.shape[1]
    row = lax.broadcasted_iota(I32, (count, entries), 0) + start
    return jnp.where(row == dest, 1.0, 0.0).astype(BF16)


def gather_rows(out_ref, dest, hi, lo, first):
    rows = out_ref.shape[0]
    step = 256
    for k in range(rows // step):
        hot = hot_rows(dest, first + k * step, step)
        total = jnp.dot(hot, hi, preferred_element_type=F32)
        total += jnp.dot(hot, lo, preferred_element_type=F32)
        out_ref[k * step : (k + 1) * step, :] = total


def main_kernel(
    a_ref, kap_ref, elev_ref, n_ref, s_ref, w_ref, e_ref, basis_ref, dest_ref, sel_ref,
    mid_ref, t_ref, b_ref, l_ref, r_ref, hi_ref, lo_ref, send_ref,
    wt, et, g_ref, y_ref, c_ref,
):
    rows, cols = a_ref.shape
    wt[...] = column(w_ref)
    et[...] = column(e_ref)

    def emit(r, x, mid):
        mid_ref[r : r + 8, :] = mid
        g = DT * (x + mid)
        for k in range(cols // 128):
            g_ref[k, r : r + 8, :] = g[:, k * 128 : (k + 1) * 128]

    stencil(a_ref, kap_ref, elev_ref, n_ref, s_ref, wt, et, emit)
    nb = rows * cols // (BS * BS)
    chunk = lax.broadcasted_iota(I32, (8, 128), 1) // BS
    for br in range(rows // BS):
        for bh in range(cols // 128):
            v = [
                g_ref[bh, pl.ds(br * BS + rl, 8, stride=4), :]
                for rl in range(4)
            ]
            for bl in range(4):
                out = v[bl]
                for rl in range(4):
                    if rl != bl:
                        moved = pltpu.roll(v[rl], ((rl - bl) * BS) % 128, 1)
                        out = jnp.where(chunk == rl, moved, out)
                b = br * (cols // BS) + bh * 4 + bl
                y_ref[pl.ds(b, 8, stride=nb), :] = out
    lhs = jnp.concatenate(
        [y_ref[rh * nb : (rh + 1) * nb, :].astype(BF16) for rh in range(8)], axis=1
    )
    products = [
        jnp.dot(lhs, basis_ref[q], preferred_element_type=F32)
        for q in range(basis_ref.shape[0])
    ]
    for o in range(4):
        sel = sel_ref[:, o : o + 1]
        out = jnp.zeros_like(products[0])
        for q, product in enumerate(products):
            out = jnp.where(sel == q, product, out)
        for h in range(2):
            c_ref[h, pl.ds(o, nb, stride=4), :] = out[:, h * 128 : (h + 1) * 128]
    contrib = jnp.concatenate([c_ref[0], c_ref[1]], axis=1)
    hi = contrib.astype(BF16)
    lo = (contrib - hi.astype(F32)).astype(BF16)
    hi_ref[...] = hi
    lo_ref[...] = lo
    gather_rows(send_ref, dest_ref[...], hi, lo, send_ref.shape[0])
    t_ref[...] = mid_ref[0:1, :]
    b_ref[...] = mid_ref[rows - 1 : rows, :]
    l_ref[...] = mid_ref[:, 0:128].T[0:1, :]
    r_ref[...] = mid_ref[:, cols - 128 : cols].T[127:128, :]


def main(a, kappa, elev, halo, basis, dest, sel, total):
    rows, cols = a.shape
    entries = dest.shape[1]
    ncoef = basis.shape[-1]
    return pl.pallas_call(
        main_kernel,
        in_specs=[vmem()] * 10,
        out_specs=[vmem()] * 8,
        out_shape=[
            whole((rows, cols)),
            whole((1, cols)),
            whole((1, cols)),
            whole((1, rows)),
            whole((1, rows)),
            jax.ShapeDtypeStruct((entries, ncoef), BF16),
            jax.ShapeDtypeStruct((entries, ncoef), BF16),
            whole((total // 2, ncoef)),
        ],
        scratch_shapes=[
            pltpu.VMEM((rows, 128), F32),
            pltpu.VMEM((rows, 128), F32),
            pltpu.VMEM((cols // 128, rows, 128), F32),
            pltpu.VMEM((rows * cols // 128, 128), F32),
            pltpu.VMEM((2, entries, 128), F32),
        ],
        compiler_params=params(),
        cost_estimate=pl.CostEstimate(
            flops=10**9, bytes_accessed=6 << 20, transcendentals=0
        ),
        name="main",
    )(a, kappa, elev, *halo, basis, dest, sel)


def keep_kernel(dest_ref, hi_ref, lo_ref, out_ref):
    gather_rows(out_ref, dest_ref[...], hi_ref[...], lo_ref[...], 0)


def keep_rows(dest, hi, lo, total):
    return pl.pallas_call(
        keep_kernel,
        in_specs=[vmem()] * 3,
        out_specs=vmem(),
        out_shape=whole((total // 2, hi.shape[1])),
        compiler_params=params(),
        cost_estimate=pl.CostEstimate(
            flops=5 * 10**8, bytes_accessed=1 << 20, transcendentals=0
        ),
        name="keep",
    )(dest, hi, lo)


def last_kernel(a_ref, kap_ref, elev_ref, n_ref, s_ref, w_ref, e_ref, out_ref, wt, et):
    wt[...] = column(w_ref)
    et[...] = column(e_ref)

    def emit(r, x, new):
        out_ref[r : r + 8, :] = new

    stencil(a_ref, kap_ref, elev_ref, n_ref, s_ref, wt, et, emit)


def last(a, kappa, elev, halo):
    rows, cols = a.shape
    return pl.pallas_call(
        last_kernel,
        in_specs=[vmem()] * 7,
        out_specs=vmem(),
        out_shape=whole((rows, cols)),
        scratch_shapes=[pltpu.VMEM((rows, 128), F32), pltpu.VMEM((rows, 128), F32)],
        compiler_params=params(),
        cost_estimate=pl.CostEstimate(
            flops=10**7, bytes_accessed=2 << 20, transcendentals=0
        ),
        name="last",
    )(a, kappa, elev, *halo)


def exchange(top, bottom, left, right):
    halo = []
    for axis, low, high in (("row", bottom, top), ("col", right, left)):
        count = lax.axis_size(axis)
        forward = [(i, i + 1) for i in range(count - 1)]
        backward = [(target, source) for source, target in forward]
        halo.append(lax.ppermute(low, axis, forward))
        halo.append(lax.ppermute(high, axis, backward))
    return halo


def partners(n_chip, distance):
    pairs = []
    for z in range(n_chip):
        for core in range(2):
            low = (z // distance) % 2 == core
            other = (z + (distance if low else -distance)) % n_chip
            pairs.append((2 * z + core, 2 * other + core))
    return pairs


def on_device(
    adj_final, kappa, elev_early, elev_late, basis, basis_index, intersection_patch, owner_row
):
    n_row = lax.axis_size("row")
    total = owner_row.shape[1]
    place = lax.axis_index("row").astype(I32)
    core, chip = place & 1, place >> 1
    halo = exchange(*edges(adj_final))
    dest, sel = indices(core.reshape(1), intersection_patch[0], owner_row, basis_index[0])
    mid, top, bottom, left, right, hi, lo, send = main(
        adj_final, kappa, elev_late, halo, basis[0, 0], dest, sel, total
    )
    got = lax.ppermute(send, "row", [(i, i ^ 1) for i in range(n_row)])
    part = keep_rows(dest, hi, lo, total) + got
    halo = exchange(top, bottom, left, right)
    adj_start = last(mid, kappa, elev_early, halo)
    distance = 1
    while distance < n_row // 2:
        half = part.shape[0] // 2
        upper = (chip // distance) & 1
        sent = lax.dynamic_slice_in_dim(part, (1 - upper) * half, half)
        got = lax.ppermute(sent, "row", partners(n_row // 2, distance))
        part = lax.dynamic_slice_in_dim(part, upper * half, half) + got
        distance *= 2
    return (adj_start, part[None])


def solution(mesh):
    return jax.shard_map(
        on_device,
        mesh=mesh,
        in_specs=(
            P(("mem", "row"), "col"),
            P(("mem", "row"), "col"),
            P(("mem", "row"), "col"),
            P(("mem", "row"), "col"),
            P(("mem", "row"), "col", None, None, None),
            P(("mem", "row"), "col", None),
            P(("mem", "row"), "col", None),
            P(("mem", "col"), None),
        ),
        out_specs=(P(("mem", "row"), "col"), P(("mem", "col"), "row", None)),
        check_vma=False,
    )
```

```python
import jax
import jax.numpy as jnp
from jax import lax
from jax.experimental import pallas as pl
from jax.experimental.pallas import tpu as pltpu
from jax.sharding import PartitionSpec as P


BS = 32
DT = 0.2
F32 = jnp.float32
BF16 = jnp.bfloat16
I32 = jnp.int32
VLIM = 24 << 20


def whole(shape):
    return jax.ShapeDtypeStruct(shape, F32)


def vmem():
    return pl.BlockSpec(memory_space=pltpu.VMEM)


def hbm():
    return pl.BlockSpec(memory_space=pltpu.HBM)


def params(limit=VLIM):
    return pltpu.CompilerParams(vmem_limit_bytes=limit)


def edges_kernel(top_ref, bot_ref, left_ref, right_ref, t_ref, b_ref, l_ref, r_ref):
    t_ref[...] = top_ref[0:1, :]
    b_ref[...] = bot_ref[7:8, :]
    l_ref[...] = left_ref[...].T[0:1, :]
    r_ref[...] = right_ref[...].T[127:128, :]


def edges(a):
    rows, cols = a.shape
    return pl.pallas_call(
        edges_kernel,
        grid=(1,),
        in_specs=[
            pl.BlockSpec((8, cols), lambda i: (0, 0)),
            pl.BlockSpec((8, cols), lambda i: (rows // 8 - 1, 0)),
            pl.BlockSpec((rows, 128), lambda i: (0, 0)),
            pl.BlockSpec((rows, 128), lambda i: (0, cols // 128 - 1)),
        ],
        out_specs=[
            pl.BlockSpec((1, cols), lambda i: (0, 0)),
            pl.BlockSpec((1, cols), lambda i: (0, 0)),
            pl.BlockSpec((1, rows), lambda i: (0, 0)),
            pl.BlockSpec((1, rows), lambda i: (0, 0)),
        ],
        out_shape=[whole((1, cols)), whole((1, cols)), whole((1, rows)), whole((1, rows))],
        compiler_params=params(4 << 20),
        name="edges",
    )(a, a, a, a)


def index_kernel(
    place_ref, patch_ref, owner_ref, idx_ref, kap_ref, elev_ref, dest_ref, sel_ref, coef_ref
):
    for r in range(0, kap_ref.shape[0], 8):
        e = elev_ref[r : r + 8, :]
        coef_ref[r : r + 8, :] = DT * kap_ref[r : r + 8, :] / (1.0 + e * e)
    entries = patch_ref.shape[1]
    patches = owner_ref.shape[1]
    hot = lax.broadcasted_iota(I32, (patches, entries), 0) == patch_ref[...]
    hot = jnp.where(hot, 1.0, 0.0).astype(BF16)
    owner = owner_ref[...]
    row = lax.broadcasted_iota(I32, (16, patches), 0)
    parts = jnp.where(row == 0, owner >> 6, jnp.where(row == 1, owner & 63, 0))
    found = jnp.dot(parts.astype(F32).astype(BF16), hot, preferred_element_type=F32)
    high = found[0:1, :].astype(I32) ^ (place_ref[0] & 3)
    low = found[1:2, :].astype(I32)
    spot = jnp.zeros_like(high)
    for bit in range(5):
        spot = spot | (((high >> bit) & 1) << (4 - bit))
    dest_ref[...] = spot * 64 + low
    nb = entries // 4
    lane = lax.broadcasted_iota(I32, (nb, entries), 1)
    block = lax.broadcasted_iota(I32, (nb, entries), 0)
    idx = jnp.broadcast_to(idx_ref[...], (nb, entries))
    for o in range(4):
        sel_ref[:, o : o + 1] = jnp.sum(
            jnp.where(lane == block * 4 + o, idx, 0), axis=1, keepdims=True
        )


def indices(place, patch, owner, idx, kappa, elev):
    entries = patch.shape[1]
    return pl.pallas_call(
        index_kernel,
        in_specs=[pl.BlockSpec(memory_space=pltpu.SMEM)] + [vmem()] * 5,
        out_specs=[vmem()] * 3,
        out_shape=[
            jax.ShapeDtypeStruct((1, entries), I32),
            jax.ShapeDtypeStruct((entries // 4, 4), I32),
            whole(kappa.shape),
        ],
        compiler_params=params(),
        name="indices",
    )(place, patch, owner, idx, kappa, elev)


def stencil(a_ref, coef_of, n_ref, s_ref, wt, et, emit):
    rows, cols = a_ref.shape
    lane = lax.broadcasted_iota(I32, (8, cols), 1)
    sub = lax.broadcasted_iota(I32, (8, cols), 0)
    for i in range(rows // 8):
        r = 8 * i
        x = a_ref[r : r + 8, :]
        if i == 0:
            up = jnp.where(sub == 0, n_ref[...], pltpu.roll(x, 1, 0))
        else:
            up = a_ref[r - 1 : r + 7, :]
        if i == rows // 8 - 1:
            down = jnp.where(sub == 7, s_ref[...], pltpu.roll(x, 7, 0))
        else:
            down = a_ref[r + 1 : r + 9, :]
        east = jnp.where(lane == cols - 1, et[r : r + 8, 0:1], pltpu.roll(x, cols - 1, 1))
        west = jnp.where(lane == 0, wt[r : r + 8, 0:1], pltpu.roll(x, 1, 1))
        lap = down + up + east + west - 4.0 * x
        emit(r, x, x + coef_of(r) * lap)


def column(ref):
    n = ref.shape[1]
    return jnp.broadcast_to(ref[...], (128, n)).T


def hot_rows(dest, start, count):
    entries = dest.shape[1]
    row = lax.broadcasted_iota(I32, (count, entries), 0) + start
    return jnp.where(row == dest, 1.0, 0.0).astype(BF16)


def gather_rows(out_ref, dest, hi, lo, first, got_ref=None):
    rows = out_ref.shape[0]
    step = 256
    for k in range(rows // step):
        hot = hot_rows(dest, first + k * step, step)
        total = jnp.dot(hot, hi, preferred_element_type=F32)
        total += jnp.dot(hot, lo, preferred_element_type=F32)
        if got_ref is not None:
            total += got_ref[first + k * step : first + (k + 1) * step, :]
        out_ref[k * step : (k + 1) * step, :] = total


def main_kernel(
    a_ref, coef_ref, n_ref, s_ref, w_ref, e_ref, basis_ref, dest_ref, sel_ref,
    mid_ref, t_ref, b_ref, l_ref, r_ref, hi_ref, lo_ref, send_ref,
    wt, et, g_ref, y_ref, c_ref, table, sem,
):
    rows, cols = a_ref.shape
    copy = pltpu.make_async_copy(basis_ref, table, sem)
    copy.start()
    wt[...] = column(w_ref)
    et[...] = column(e_ref)

    def emit(r, x, mid):
        mid_ref[r : r + 8, :] = mid
        g = DT * (x + mid)
        for k in range(cols // 128):
            g_ref[k, r : r + 8, :] = g[:, k * 128 : (k + 1) * 128]

    stencil(a_ref, lambda r: coef_ref[r : r + 8, :], n_ref, s_ref, wt, et, emit)
    nb = rows * cols // (BS * BS)
    chunk = lax.broadcasted_iota(I32, (8, 128), 1) // BS
    for br in range(rows // BS):
        for bh in range(cols // 128):
            v = [
                g_ref[bh, pl.ds(br * BS + rl, 8, stride=4), :]
                for rl in range(4)
            ]
            for bl in range(4):
                out = v[bl]
                for rl in range(4):
                    if rl != bl:
                        moved = pltpu.roll(v[rl], ((rl - bl) * BS) % 128, 1)
                        out = jnp.where(chunk == rl, moved, out)
                b = br * (cols // BS) + bh * 4 + bl
                y_ref[pl.ds(b, 8, stride=nb), :] = out
    lhs = jnp.concatenate(
        [y_ref[rh * nb : (rh + 1) * nb, :].astype(BF16) for rh in range(8)], axis=1
    )
    copy.wait()
    products = [
        jnp.dot(lhs, table[q], preferred_element_type=F32)
        for q in range(basis_ref.shape[0])
    ]
    for o in range(4):
        sel = sel_ref[:, o : o + 1]
        out = jnp.zeros_like(products[0])
        for q, product in enumerate(products):
            out = jnp.where(sel == q, product, out)
        for h in range(2):
            c_ref[h, pl.ds(o, nb, stride=4), :] = out[:, h * 128 : (h + 1) * 128]
    contrib = jnp.concatenate([c_ref[0], c_ref[1]], axis=1)
    hi = contrib.astype(BF16)
    lo = (contrib - hi.astype(F32)).astype(BF16)
    hi_ref[...] = hi
    lo_ref[...] = lo
    gather_rows(send_ref, dest_ref[...], hi, lo, send_ref.shape[0])
    t_ref[...] = mid_ref[0:1, :]
    b_ref[...] = mid_ref[rows - 1 : rows, :]
    l_ref[...] = mid_ref[:, 0:128].T[0:1, :]
    r_ref[...] = mid_ref[:, cols - 128 : cols].T[127:128, :]


def main(a, coef, halo, basis, dest, sel, total):
    rows, cols = a.shape
    entries = dest.shape[1]
    ncoef = basis.shape[-1]
    return pl.pallas_call(
        main_kernel,
        in_specs=[vmem()] * 6 + [hbm()] + [vmem()] * 2,
        out_specs=[vmem()] * 8,
        out_shape=[
            whole((rows, cols)),
            whole((1, cols)),
            whole((1, cols)),
            whole((1, rows)),
            whole((1, rows)),
            jax.ShapeDtypeStruct((entries, ncoef), BF16),
            jax.ShapeDtypeStruct((entries, ncoef), BF16),
            whole((total // 2, ncoef)),
        ],
        scratch_shapes=[
            pltpu.VMEM((rows, 128), F32),
            pltpu.VMEM((rows, 128), F32),
            pltpu.VMEM((cols // 128, rows, 128), F32),
            pltpu.VMEM((rows * cols // 128, 128), F32),
            pltpu.VMEM((2, entries, 128), F32),
            pltpu.VMEM(basis.shape, BF16),
            pltpu.SemaphoreType.DMA,
        ],
        compiler_params=params(),
        cost_estimate=pl.CostEstimate(
            flops=10**9, bytes_accessed=6 << 20, transcendentals=0
        ),
        name="main",
    )(a, coef, *halo, basis, dest, sel)


def keep_kernel(dest_ref, hi_ref, lo_ref, got_ref, sent_ref, part_ref):
    dest, hi, lo = dest_ref[...], hi_ref[...], lo_ref[...]
    half = part_ref.shape[0]
    gather_rows(sent_ref, dest, hi, lo, half, got_ref)
    gather_rows(part_ref, dest, hi, lo, 0, got_ref)


def keep_rows(dest, hi, lo, got):
    half = whole((got.shape[0] // 2, got.shape[1]))
    return pl.pallas_call(
        keep_kernel,
        in_specs=[vmem()] * 4,
        out_specs=[vmem()] * 2,
        out_shape=[half, half],
        compiler_params=params(),
        cost_estimate=pl.CostEstimate(
            flops=5 * 10**8, bytes_accessed=1 << 20, transcendentals=0
        ),
        name="keep",
    )(dest, hi, lo, got)


def last_kernel(
    a_ref, kap_hbm, elev_hbm, n_ref, s_ref, w_ref, e_ref, out_ref, kap, elev, wt, et, sems
):
    copies = [
        pltpu.make_async_copy(kap_hbm, kap, sems.at[0]),
        pltpu.make_async_copy(elev_hbm, elev, sems.at[1]),
    ]
    for copy in copies:
        copy.start()
    wt[...] = column(w_ref)
    et[...] = column(e_ref)
    for copy in copies:
        copy.wait()

    def emit(r, x, new):
        out_ref[r : r + 8, :] = new

    def coef(r):
        e = elev[r : r + 8, :]
        return DT * kap[r : r + 8, :] / (1.0 + e * e)

    stencil(a_ref, coef, n_ref, s_ref, wt, et, emit)


def last(a, kappa, elev, halo):
    rows, cols = a.shape
    return pl.pallas_call(
        last_kernel,
        in_specs=[vmem(), hbm(), hbm()] + [vmem()] * 4,
        out_specs=vmem(),
        out_shape=whole((rows, cols)),
        scratch_shapes=[
            pltpu.VMEM((rows, cols), F32),
            pltpu.VMEM((rows, cols), F32),
            pltpu.VMEM((rows, 128), F32),
            pltpu.VMEM((rows, 128), F32),
            pltpu.SemaphoreType.DMA((2,)),
        ],
        compiler_params=params(),
        cost_estimate=pl.CostEstimate(
            flops=10**7, bytes_accessed=2 << 20, transcendentals=0
        ),
        name="last",
    )(a, kappa, elev, *halo)


def exchange(axis, low, high):
    count = lax.axis_size(axis)
    forward = [(i, i + 1) for i in range(count - 1)]
    backward = [(target, source) for source, target in forward]
    return [lax.ppermute(low, axis, forward), lax.ppermute(high, axis, backward)]


def partners(n_chip, distance):
    pairs = []
    for z in range(n_chip):
        for core in range(2):
            low = (z // distance) % 2 == core
            other = (z + (distance if low else -distance)) % n_chip
            pairs.append((2 * z + core, 2 * other + core))
    return pairs


def compute(
    adj_final, kappa, elev_early, elev_late, basis, basis_index, intersection_patch, owner_row
):
    n_row = lax.axis_size("row")
    total = owner_row.shape[1]
    place = lax.axis_index("row").astype(I32)
    chip = place >> 1
    top, bottom, left, right = edges(adj_final)
    halo = exchange("row", bottom, top) + exchange("col", right, left)
    dest, sel, coef = indices(
        place.reshape(1), intersection_patch[0], owner_row, basis_index[0], kappa, elev_late
    )
    mid, top, bottom, left, right, hi, lo, send = main(
        adj_final, coef, halo, basis[0, 0], dest, sel, total
    )
    got = lax.ppermute(send, "row", [(i, i ^ 1) for i in range(n_row)])
    sent, part = keep_rows(dest, hi, lo, got)
    halo_col = exchange("col", right, left)
    halo_row = exchange("row", bottom, top)
    adj_start = last(mid, kappa, elev_early, halo_row + halo_col)
    distance = 1
    while True:
        got = lax.ppermute(sent, "row", partners(n_row // 2, distance))
        total = part + got
        distance *= 2
        if distance == n_row // 2:
            return (adj_start, total[None])
        half = total.shape[0] // 2
        upper = (chip // distance) & 1
        sent = lax.dynamic_slice_in_dim(total, (1 - upper) * half, half)
        part = lax.dynamic_slice_in_dim(total, upper * half, half)


def solution(mesh):
    return jax.shard_map(
        compute,
        mesh=mesh,
        in_specs=(
            P(("mem", "row"), "col"),
            P(("mem", "row"), "col"),
            P(("mem", "row"), "col"),
            P(("mem", "row"), "col"),
            P(("mem", "row"), "col", None, None, None),
            P(("mem", "row"), "col", None),
            P(("mem", "row"), "col", None),
            P(("mem", "col"), None),
        ),
        out_specs=(P(("mem", "row"), "col"), P(("mem", "col"), "row", None)),
        check_vma=False,
    )
```

```python
import functools

import jax
import jax.numpy as jnp
from jax import lax
from jax.experimental import pallas as pl
from jax.experimental.pallas import tpu as pltpu
from jax.sharding import PartitionSpec as P


BS = 32
DT = 0.2
F32 = jnp.float32
BF16 = jnp.bfloat16
I32 = jnp.int32
VLIM = 24 << 20


def whole(shape):
    return jax.ShapeDtypeStruct(shape, F32)


def vmem():
    return pl.BlockSpec(memory_space=pltpu.VMEM)


def hbm():
    return pl.BlockSpec(memory_space=pltpu.HBM)


def in_hbm(x):
    return pltpu.with_memory_space_constraint(x, pltpu.HBM)


def params(limit=VLIM):
    return pltpu.CompilerParams(vmem_limit_bytes=limit)


def edge_row(x, inner, kap, elev):
    lane = lax.broadcasted_iota(I32, x.shape, 1)
    last = x.shape[1] - 1
    east = jnp.where(lane == last, 0.0, pltpu.roll(x, last, 1))
    west = jnp.where(lane == 0, 0.0, pltpu.roll(x, 1, 1))
    coef = DT * kap / (1.0 + elev * elev)
    return x + coef * (inner + east + west - 4.0 * x), coef


def edges_kernel(
    top_ref, bot_ref, left_ref, right_ref, ktop_ref, kbot_ref, etop_ref, ebot_ref,
    t_ref, b_ref, l_ref, r_ref,
):
    top, bot = top_ref[...], bot_ref[...]
    partial, coef = edge_row(top, pltpu.roll(top, 7, 0), ktop_ref[...], etop_ref[...])
    t_ref[0:1, :] = top[0:1, :]
    t_ref[1:2, :] = partial[0:1, :]
    t_ref[2:3, :] = coef[0:1, :]
    partial, coef = edge_row(bot, pltpu.roll(bot, 1, 0), kbot_ref[...], ebot_ref[...])
    b_ref[0:1, :] = bot[7:8, :]
    b_ref[1:2, :] = partial[7:8, :]
    b_ref[2:3, :] = coef[7:8, :]
    l_ref[...] = left_ref[...].T[0:1, :]
    r_ref[...] = right_ref[...].T[127:128, :]


def edges(a, kappa, elev):
    rows, cols = a.shape
    first = pl.BlockSpec((8, cols), lambda i: (0, 0))
    final = pl.BlockSpec((8, cols), lambda i: (rows // 8 - 1, 0))
    return pl.pallas_call(
        edges_kernel,
        grid=(1,),
        in_specs=[
            first,
            final,
            pl.BlockSpec((rows, 128), lambda i: (0, 0)),
            pl.BlockSpec((rows, 128), lambda i: (0, cols // 128 - 1)),
            first,
            final,
            first,
            final,
        ],
        out_specs=[
            pl.BlockSpec((3, cols), lambda i: (0, 0)),
            pl.BlockSpec((3, cols), lambda i: (0, 0)),
            pl.BlockSpec((1, rows), lambda i: (0, 0)),
            pl.BlockSpec((1, rows), lambda i: (0, 0)),
        ],
        out_shape=[whole((3, cols)), whole((3, cols)), whole((1, rows)), whole((1, rows))],
        compiler_params=params(4 << 20),
        name="edges",
    )(a, a, a, a, kappa, kappa, elev, elev)


def index_kernel(
    place_ref, patch_ref, owner_ref, idx_ref, kap_ref, elev_ref, dest_ref, sel_ref, coef_ref
):
    for r in range(0, kap_ref.shape[0], 8):
        e = elev_ref[r : r + 8, :]
        coef_ref[r : r + 8, :] = DT * kap_ref[r : r + 8, :] / (1.0 + e * e)
    entries = patch_ref.shape[1]
    patches = owner_ref.shape[1]
    hot = lax.broadcasted_iota(I32, (patches, entries), 0) == patch_ref[...]
    hot = jnp.where(hot, 1.0, 0.0).astype(BF16)
    owner = owner_ref[...]
    row = lax.broadcasted_iota(I32, (16, patches), 0)
    parts = jnp.where(row == 0, owner >> 6, jnp.where(row == 1, owner & 63, 0))
    found = jnp.dot(parts.astype(F32).astype(BF16), hot, preferred_element_type=F32)
    high = found[0:1, :].astype(I32) ^ (place_ref[0] & 3)
    low = found[1:2, :].astype(I32)
    spot = jnp.zeros_like(high)
    for bit in range(5):
        spot = spot | (((high >> bit) & 1) << (4 - bit))
    dest_ref[...] = spot * 64 + low
    nb = entries // 4
    lane = lax.broadcasted_iota(I32, (nb, entries), 1)
    block = lax.broadcasted_iota(I32, (nb, entries), 0)
    idx = jnp.broadcast_to(idx_ref[...], (nb, entries))
    for o in range(4):
        sel_ref[:, o : o + 1] = jnp.sum(
            jnp.where(lane == block * 4 + o, idx, 0), axis=1, keepdims=True
        )


def indices(place, patch, owner, idx, kappa, elev):
    entries = patch.shape[1]
    return pl.pallas_call(
        index_kernel,
        in_specs=[pl.BlockSpec(memory_space=pltpu.SMEM)] + [vmem()] * 5,
        out_specs=[vmem()] * 3,
        out_shape=[
            jax.ShapeDtypeStruct((1, entries), I32),
            jax.ShapeDtypeStruct((entries // 4, 4), I32),
            whole(kappa.shape),
        ],
        compiler_params=params(),
        name="indices",
    )(place, patch, owner, idx, kappa, elev)


def stencil(a_ref, coef_of, north, south, wt, et, emit):
    rows, cols = a_ref.shape
    lane = lax.broadcasted_iota(I32, (8, cols), 1)
    sub = lax.broadcasted_iota(I32, (8, cols), 0)
    for i in range(rows // 8):
        r = 8 * i
        x = a_ref[r : r + 8, :]
        if i == 0:
            up = jnp.where(sub == 0, north, pltpu.roll(x, 1, 0))
        else:
            up = a_ref[r - 1 : r + 7, :]
        if i == rows // 8 - 1:
            down = jnp.where(sub == 7, south, pltpu.roll(x, 7, 0))
        else:
            down = a_ref[r + 1 : r + 9, :]
        east = jnp.where(lane == cols - 1, et[r : r + 8, 0:1], pltpu.roll(x, cols - 1, 1))
        west = jnp.where(lane == 0, wt[r : r + 8, 0:1], pltpu.roll(x, 1, 1))
        lap = down + up + east + west - 4.0 * x
        emit(r, x, x + coef_of(r) * lap)


def column(ref):
    return jnp.broadcast_to(ref[:, 0:128], (128, 128)).T


def hot_rows(dest, start, count):
    entries = dest.shape[1]
    row = lax.broadcasted_iota(I32, (count, entries), 0) + start
    return jnp.where(row == dest, 1.0, 0.0).astype(BF16)


def gather_rows(out_ref, dest, hi, lo, first, got_ref=None):
    rows = out_ref.shape[0]
    step = 256
    for k in range(rows // step):
        hot = hot_rows(dest, first + k * step, step)
        total = jnp.dot(hot, hi, preferred_element_type=F32)
        total += jnp.dot(hot, lo, preferred_element_type=F32)
        if got_ref is not None:
            total += got_ref[first + k * step : first + (k + 1) * step, :]
        out_ref[k * step : (k + 1) * step, :] = total


def main_kernel(
    a_ref, coef_ref, n_ref, s_ref, w_ref, e_ref, basis_ref, dest_ref, sel_ref,
    mid_hbm, l_ref, r_ref, hi_ref, lo_ref, send_ref,
    wt, et, g_ref, y_ref, c_ref, table, mid_ref, sems,
):
    rows, cols = a_ref.shape
    copy = pltpu.make_async_copy(basis_ref, table, sems.at[0])
    copy.start()
    wt[...] = column(w_ref)
    et[...] = column(e_ref)

    def emit(r, x, mid):
        mid_ref[r : r + 8, :] = mid
        g = DT * (x + mid)
        for k in range(cols // 128):
            g_ref[k, r : r + 8, :] = g[:, k * 128 : (k + 1) * 128]

    north, south = n_ref[0:1, :], s_ref[0:1, :]
    stencil(a_ref, lambda r: coef_ref[r : r + 8, :], north, south, wt, et, emit)
    stored = pltpu.make_async_copy(mid_ref, mid_hbm, sems.at[1])
    stored.start()
    nb = rows * cols // (BS * BS)
    chunk = lax.broadcasted_iota(I32, (8, 128), 1) // BS
    for br in range(rows // BS):
        for bh in range(cols // 128):
            v = [
                g_ref[bh, pl.ds(br * BS + rl, 8, stride=4), :]
                for rl in range(4)
            ]
            for bl in range(4):
                out = v[bl]
                for rl in range(4):
                    if rl != bl:
                        moved = pltpu.roll(v[rl], ((rl - bl) * BS) % 128, 1)
                        out = jnp.where(chunk == rl, moved, out)
                b = br * (cols // BS) + bh * 4 + bl
                y_ref[pl.ds(b, 8, stride=nb), :] = out
    lhs = jnp.concatenate(
        [y_ref[rh * nb : (rh + 1) * nb, :].astype(BF16) for rh in range(8)], axis=1
    )
    copy.wait()
    products = [
        jnp.dot(lhs, table[q], preferred_element_type=F32)
        for q in range(basis_ref.shape[0])
    ]
    for o in range(4):
        sel = sel_ref[:, o : o + 1]
        out = jnp.zeros_like(products[0])
        for q, product in enumerate(products):
            out = jnp.where(sel == q, product, out)
        for h in range(2):
            c_ref[h, pl.ds(o, nb, stride=4), :] = out[:, h * 128 : (h + 1) * 128]
    contrib = jnp.concatenate([c_ref[0], c_ref[1]], axis=1)
    hi = contrib.astype(BF16)
    lo = (contrib - hi.astype(F32)).astype(BF16)
    hi_ref[...] = hi
    lo_ref[...] = lo
    gather_rows(send_ref, dest_ref[...], hi, lo, send_ref.shape[0])
    l_ref[:, 0:128] = mid_ref[:, 0:128].T[0:1, :]
    r_ref[:, 0:128] = mid_ref[:, cols - 128 : cols].T[127:128, :]
    lane = lax.broadcasted_iota(I32, (1, 128), 1)
    for out, k in ((l_ref, 0), (r_ref, cols - 1)):
        corner = jnp.where(lane == 1, south[:, k : k + 1], 0.0)
        out[:, 128:256] = jnp.where(lane == 0, north[:, k : k + 1], corner)
    stored.wait()


def main(a, coef, halo, basis, dest, sel, total):
    rows, cols = a.shape
    entries = dest.shape[1]
    ncoef = basis.shape[-1]
    return pl.pallas_call(
        main_kernel,
        in_specs=[vmem()] * 6 + [hbm()] + [vmem()] * 2,
        out_specs=[hbm()] + [vmem()] * 5,
        out_shape=[
            whole((rows, cols)),
            whole((1, 2 * rows)),
            whole((1, 2 * rows)),
            jax.ShapeDtypeStruct((entries, ncoef), BF16),
            jax.ShapeDtypeStruct((entries, ncoef), BF16),
            whole((total // 2, ncoef)),
        ],
        scratch_shapes=[
            pltpu.VMEM((rows, 128), F32),
            pltpu.VMEM((rows, 128), F32),
            pltpu.VMEM((cols // 128, rows, 128), F32),
            pltpu.VMEM((rows * cols // 128, 128), F32),
            pltpu.VMEM((2, entries, 128), F32),
            pltpu.VMEM(basis.shape, BF16),
            pltpu.VMEM((rows, cols), F32),
            pltpu.SemaphoreType.DMA((2,)),
        ],
        compiler_params=params(),
        cost_estimate=pl.CostEstimate(
            flops=10**9, bytes_accessed=6 << 20, transcendentals=0
        ),
        name="main",
    )(a, coef, *halo, basis, dest, sel)


def add_kernel(first, dest_ref, hi_ref, lo_ref, got_ref, out_ref):
    gather_rows(out_ref, dest_ref[...], hi_ref[...], lo_ref[...], first, got_ref)


def add_rows(first, count, dest, hi, lo, got):
    ncoef = got.shape[1]
    return pl.pallas_call(
        functools.partial(add_kernel, first),
        in_specs=[vmem()] * 4,
        out_specs=vmem(),
        out_shape=whole((count, ncoef)),
        compiler_params=params(),
        cost_estimate=pl.CostEstimate(
            flops=3 * 10**8, bytes_accessed=1 << 20, transcendentals=0
        ),
        name="add",
    )(dest, hi, lo, got)


def last_kernel(
    a_hbm, kap_hbm, elev_hbm, n_ref, s_ref, w_ref, e_ref, t_ref, b_ref, out_ref,
    a_ref, kap, elev, wt, et, sems,
):
    copies = [
        pltpu.make_async_copy(a_hbm, a_ref, sems.at[2]),
        pltpu.make_async_copy(kap_hbm, kap, sems.at[0]),
        pltpu.make_async_copy(elev_hbm, elev, sems.at[1]),
    ]
    for copy in copies:
        copy.start()
    wt[...] = column(w_ref)
    et[...] = column(e_ref)
    for copy in copies:
        copy.wait()

    def emit(r, x, new):
        out_ref[r : r + 8, :] = new

    def coef(r):
        e = elev[r : r + 8, :]
        return DT * kap[r : r + 8, :] / (1.0 + e * e)

    lane = lax.broadcasted_iota(I32, (1, a_ref.shape[1]), 1)
    beyond = []
    for k, (ref, own) in enumerate(((n_ref, t_ref), (s_ref, b_ref))):
        missing = own[0:1, :]
        missing += jnp.where(lane == 0, w_ref[:, 128 + k : 129 + k], 0.0)
        missing += jnp.where(lane == a_ref.shape[1] - 1, e_ref[:, 128 + k : 129 + k], 0.0)
        beyond.append(ref[1:2, :] + ref[2:3, :] * missing)
    stencil(a_ref, coef, *beyond, wt, et, emit)


def last(a, kappa, elev, halo, own):
    rows, cols = a.shape
    return pl.pallas_call(
        last_kernel,
        in_specs=[hbm()] * 3 + [vmem()] * 6,
        out_specs=vmem(),
        out_shape=whole((rows, cols)),
        scratch_shapes=[
            pltpu.VMEM((rows, cols), F32),
            pltpu.VMEM((rows, cols), F32),
            pltpu.VMEM((rows, cols), F32),
            pltpu.VMEM((rows, 128), F32),
            pltpu.VMEM((rows, 128), F32),
            pltpu.SemaphoreType.DMA((3,)),
        ],
        compiler_params=params(),
        cost_estimate=pl.CostEstimate(
            flops=10**7, bytes_accessed=2 << 20, transcendentals=0
        ),
        name="last",
    )(a, kappa, elev, *halo, *own)


def exchange(axis, low, high):
    count = lax.axis_size(axis)
    forward = [(i, i + 1) for i in range(count - 1)]
    backward = [(target, source) for source, target in forward]
    return [lax.ppermute(low, axis, forward), lax.ppermute(high, axis, backward)]


def partners(n_chip, distance):
    pairs = []
    for z in range(n_chip):
        for core in range(2):
            low = (z // distance) % 2 == core
            other = (z + (distance if low else -distance)) % n_chip
            pairs.append((2 * z + core, 2 * other + core))
    return pairs


def compute(
    adj_final, kappa, elev_early, elev_late, basis, basis_index, intersection_patch, owner_row
):
    n_row = lax.axis_size("row")
    total = owner_row.shape[1]
    place = lax.axis_index("row").astype(I32)
    chip = place >> 1
    top, bottom, left, right = edges(in_hbm(adj_final), in_hbm(kappa), in_hbm(elev_late))
    halo_row = exchange("row", bottom, top)
    halo = halo_row + exchange("col", right, left)
    dest, sel, coef = indices(
        place.reshape(1), intersection_patch[0], owner_row, basis_index[0], kappa, elev_late
    )
    mid, left, right, hi, lo, send = main(
        adj_final, coef, halo, in_hbm(basis[0, 0]), dest, sel, total
    )
    got = lax.ppermute(send, "row", [(i, i ^ 1) for i in range(n_row)])
    half = got.shape[0] // 2
    sent = add_rows(half, half, dest, hi, lo, got)
    part = add_rows(0, half, dest, hi, lo, got)
    halo_col = exchange("col", right, left)
    adj_start = last(mid, in_hbm(kappa), in_hbm(elev_early), halo_row + halo_col, (top, bottom))
    distance = 1
    while True:
        got = lax.ppermute(sent, "row", partners(n_row // 2, distance))
        total = part + got
        distance *= 2
        if distance == n_row // 2:
            return (adj_start, total[None])
        half = total.shape[0] // 2
        upper = (chip // distance) & 1
        sent = lax.dynamic_slice_in_dim(total, (1 - upper) * half, half)
        part = lax.dynamic_slice_in_dim(total, upper * half, half)


def solution(mesh):
    return jax.shard_map(
        compute,
        mesh=mesh,
        in_specs=(
            P(("mem", "row"), "col"),
            P(("mem", "row"), "col"),
            P(("mem", "row"), "col"),
            P(("mem", "row"), "col"),
            P(("mem", "row"), "col", None, None, None),
            P(("mem", "row"), "col", None),
            P(("mem", "row"), "col", None),
            P(("mem", "col"), None),
        ),
        out_specs=(P(("mem", "row"), "col"), P(("mem", "col"), "row", None)),
        check_vma=False,
    )
```

```python
import functools

import jax
import jax.numpy as jnp
from jax import lax
from jax.experimental import pallas as pl
from jax.experimental.pallas import tpu as pltpu
from jax.sharding import PartitionSpec as P


BS = 32
DT = 0.2
F32 = jnp.float32
BF16 = jnp.bfloat16
I32 = jnp.int32
VLIM = 24 << 20


def whole(shape):
    return jax.ShapeDtypeStruct(shape, F32)


def vmem():
    return pl.BlockSpec(memory_space=pltpu.VMEM)


def hbm():
    return pl.BlockSpec(memory_space=pltpu.HBM)


def in_hbm(x):
    return pltpu.with_memory_space_constraint(x, pltpu.HBM)


def params(limit=VLIM):
    return pltpu.CompilerParams(vmem_limit_bytes=limit)


def paths(n_chip):
    steps = n_chip.bit_length() - 1
    spots = [0] * n_chip
    for path in range(n_chip):
        at = 0
        for step in range(steps):
            if (path >> (steps - 1 - step)) & 1:
                at += -swing(step) if at % 2 else swing(step)
        spots[at % n_chip] = path
    return spots


def edge_row(x, inner, kap, elev):
    lane = lax.broadcasted_iota(I32, x.shape, 1)
    last = x.shape[1] - 1
    east = jnp.where(lane == last, 0.0, pltpu.roll(x, last, 1))
    west = jnp.where(lane == 0, 0.0, pltpu.roll(x, 1, 1))
    coef = DT * kap / (1.0 + elev * elev)
    return x + coef * (inner + east + west - 4.0 * x), coef


def edges_kernel(
    top_ref, bot_ref, left_ref, right_ref, ktop_ref, kbot_ref, etop_ref, ebot_ref,
    t_ref, b_ref, l_ref, r_ref,
):
    top, bot = top_ref[...], bot_ref[...]
    partial, coef = edge_row(top, pltpu.roll(top, 7, 0), ktop_ref[...], etop_ref[...])
    t_ref[0:1, :] = top[0:1, :]
    t_ref[1:2, :] = partial[0:1, :]
    t_ref[2:3, :] = coef[0:1, :]
    partial, coef = edge_row(bot, pltpu.roll(bot, 1, 0), kbot_ref[...], ebot_ref[...])
    b_ref[0:1, :] = bot[7:8, :]
    b_ref[1:2, :] = partial[7:8, :]
    b_ref[2:3, :] = coef[7:8, :]
    l_ref[...] = left_ref[...].T[0:1, :]
    r_ref[...] = right_ref[...].T[127:128, :]


def edges(a, kappa, elev):
    rows, cols = a.shape
    first = pl.BlockSpec((8, cols), lambda i: (0, 0))
    final = pl.BlockSpec((8, cols), lambda i: (rows // 8 - 1, 0))
    return pl.pallas_call(
        edges_kernel,
        grid=(1,),
        in_specs=[
            first,
            final,
            pl.BlockSpec((rows, 128), lambda i: (0, 0)),
            pl.BlockSpec((rows, 128), lambda i: (0, cols // 128 - 1)),
            first,
            final,
            first,
            final,
        ],
        out_specs=[
            pl.BlockSpec((3, cols), lambda i: (0, 0)),
            pl.BlockSpec((3, cols), lambda i: (0, 0)),
            pl.BlockSpec((1, rows), lambda i: (0, 0)),
            pl.BlockSpec((1, rows), lambda i: (0, 0)),
        ],
        out_shape=[whole((3, cols)), whole((3, cols)), whole((1, rows)), whole((1, rows))],
        compiler_params=params(4 << 20),
        name="edges",
    )(a, a, a, a, kappa, kappa, elev, elev)


def index_kernel(
    place_ref, patch_ref, owner_ref, idx_ref, kap_ref, elev_ref, dest_ref, sel_ref, coef_ref
):
    for r in range(0, kap_ref.shape[0], 8):
        e = elev_ref[r : r + 8, :]
        coef_ref[r : r + 8, :] = DT * kap_ref[r : r + 8, :] / (1.0 + e * e)
    entries = patch_ref.shape[1]
    patches = owner_ref.shape[1]
    hot = lax.broadcasted_iota(I32, (patches, entries), 0) == patch_ref[...]
    hot = jnp.where(hot, 1.0, 0.0).astype(BF16)
    owner = owner_ref[...]
    row = lax.broadcasted_iota(I32, (16, patches), 0)
    parts = jnp.where(row == 0, owner >> 6, jnp.where(row == 1, owner & 63, 0))
    found = jnp.dot(parts.astype(F32).astype(BF16), hot, preferred_element_type=F32)
    high = found[0:1, :].astype(I32)
    core, chip = place_ref[0] & 1, place_ref[0] >> 1
    n_chip = patches // 128
    mirror = (chip + high) & 1
    away = (high >> 1) - chip
    away = jnp.where(mirror == 1, -away, away) & (n_chip - 1)
    low = found[1:2, :].astype(I32)
    spot = ((high & 1) ^ core) * n_chip
    for d, path in enumerate(paths(n_chip)):
        spot += jnp.where(away == d, path, 0)
    dest_ref[...] = spot * 64 + low
    nb = entries // 4
    lane = lax.broadcasted_iota(I32, (nb, entries), 1)
    block = lax.broadcasted_iota(I32, (nb, entries), 0)
    idx = jnp.broadcast_to(idx_ref[...], (nb, entries))
    for o in range(4):
        sel_ref[:, o : o + 1] = jnp.sum(
            jnp.where(lane == block * 4 + o, idx, 0), axis=1, keepdims=True
        )


def indices(place, patch, owner, idx, kappa, elev):
    entries = patch.shape[1]
    return pl.pallas_call(
        index_kernel,
        in_specs=[pl.BlockSpec(memory_space=pltpu.SMEM)] + [vmem()] * 5,
        out_specs=[vmem()] * 3,
        out_shape=[
            jax.ShapeDtypeStruct((1, entries), I32),
            jax.ShapeDtypeStruct((entries // 4, 4), I32),
            whole(kappa.shape),
        ],
        compiler_params=params(),
        name="indices",
    )(place, patch, owner, idx, kappa, elev)


def stencil(a_ref, coef_of, north, south, wt, et, emit):
    rows, cols = a_ref.shape
    lane = lax.broadcasted_iota(I32, (8, cols), 1)
    sub = lax.broadcasted_iota(I32, (8, cols), 0)
    for i in range(rows // 8):
        r = 8 * i
        x = a_ref[r : r + 8, :]
        if i == 0:
            up = jnp.where(sub == 0, north, pltpu.roll(x, 1, 0))
        else:
            up = a_ref[r - 1 : r + 7, :]
        if i == rows // 8 - 1:
            down = jnp.where(sub == 7, south, pltpu.roll(x, 7, 0))
        else:
            down = a_ref[r + 1 : r + 9, :]
        east = jnp.where(lane == cols - 1, et[r : r + 8, 0:1], pltpu.roll(x, cols - 1, 1))
        west = jnp.where(lane == 0, wt[r : r + 8, 0:1], pltpu.roll(x, 1, 1))
        lap = down + up + east + west - 4.0 * x
        emit(r, x, x + coef_of(r) * lap)


def column(ref):
    return jnp.broadcast_to(ref[:, 0:128], (128, 128)).T


def hot_rows(dest, start, count):
    entries = dest.shape[1]
    row = lax.broadcasted_iota(I32, (count, entries), 0) + start
    return jnp.where(row == dest, 1.0, 0.0).astype(BF16)


def gather_rows(out_ref, dest, hi, lo, first, got_ref=None):
    rows = out_ref.shape[0]
    step = 256
    for k in range(rows // step):
        hot = hot_rows(dest, first + k * step, step)
        total = jnp.dot(hot, hi, preferred_element_type=F32)
        total += jnp.dot(hot, lo, preferred_element_type=F32)
        if got_ref is not None:
            total += got_ref[first + k * step : first + (k + 1) * step, :]
        out_ref[k * step : (k + 1) * step, :] = total


def main_kernel(
    a_ref, coef_ref, n_ref, s_ref, w_ref, e_ref, basis_ref, dest_ref, sel_ref,
    mid_hbm, l_ref, r_ref, hi_ref, lo_ref, send_ref,
    wt, et, g_ref, y_ref, c_ref, table, mid_ref, sems,
):
    rows, cols = a_ref.shape
    copy = pltpu.make_async_copy(basis_ref, table, sems.at[0])
    copy.start()
    wt[...] = column(w_ref)
    et[...] = column(e_ref)

    def emit(r, x, mid):
        mid_ref[r : r + 8, :] = mid
        g = DT * (x + mid)
        for k in range(cols // 128):
            g_ref[k, r : r + 8, :] = g[:, k * 128 : (k + 1) * 128]

    north, south = n_ref[0:1, :], s_ref[0:1, :]
    stencil(a_ref, lambda r: coef_ref[r : r + 8, :], north, south, wt, et, emit)
    stored = pltpu.make_async_copy(mid_ref, mid_hbm, sems.at[1])
    stored.start()
    nb = rows * cols // (BS * BS)
    chunk = lax.broadcasted_iota(I32, (8, 128), 1) // BS
    for br in range(rows // BS):
        for bh in range(cols // 128):
            v = [
                g_ref[bh, pl.ds(br * BS + rl, 8, stride=4), :]
                for rl in range(4)
            ]
            for bl in range(4):
                out = v[bl]
                for rl in range(4):
                    if rl != bl:
                        moved = pltpu.roll(v[rl], ((rl - bl) * BS) % 128, 1)
                        out = jnp.where(chunk == rl, moved, out)
                b = br * (cols // BS) + bh * 4 + bl
                y_ref[pl.ds(b, 8, stride=nb), :] = out
    lhs = jnp.concatenate(
        [y_ref[rh * nb : (rh + 1) * nb, :].astype(BF16) for rh in range(8)], axis=1
    )
    copy.wait()
    products = [
        jnp.dot(lhs, table[q], preferred_element_type=F32)
        for q in range(basis_ref.shape[0])
    ]
    for o in range(4):
        sel = sel_ref[:, o : o + 1]
        out = jnp.zeros_like(products[0])
        for q, product in enumerate(products):
            out = jnp.where(sel == q, product, out)
        for h in range(2):
            c_ref[h, pl.ds(o, nb, stride=4), :] = out[:, h * 128 : (h + 1) * 128]
    contrib = jnp.concatenate([c_ref[0], c_ref[1]], axis=1)
    hi = contrib.astype(BF16)
    lo = (contrib - hi.astype(F32)).astype(BF16)
    hi_ref[...] = hi
    lo_ref[...] = lo
    gather_rows(send_ref, dest_ref[...], hi, lo, send_ref.shape[0])
    l_ref[:, 0:128] = mid_ref[:, 0:128].T[0:1, :]
    r_ref[:, 0:128] = mid_ref[:, cols - 128 : cols].T[127:128, :]
    lane = lax.broadcasted_iota(I32, (1, 128), 1)
    for out, k in ((l_ref, 0), (r_ref, cols - 1)):
        corner = jnp.where(lane == 1, south[:, k : k + 1], 0.0)
        out[:, 128:256] = jnp.where(lane == 0, north[:, k : k + 1], corner)
    stored.wait()


def main(a, coef, halo, basis, dest, sel, total):
    rows, cols = a.shape
    entries = dest.shape[1]
    ncoef = basis.shape[-1]
    return pl.pallas_call(
        main_kernel,
        in_specs=[vmem()] * 6 + [hbm()] + [vmem()] * 2,
        out_specs=[hbm()] + [vmem()] * 5,
        out_shape=[
            whole((rows, cols)),
            whole((1, 2 * rows)),
            whole((1, 2 * rows)),
            jax.ShapeDtypeStruct((entries, ncoef), BF16),
            jax.ShapeDtypeStruct((entries, ncoef), BF16),
            whole((total // 2, ncoef)),
        ],
        scratch_shapes=[
            pltpu.VMEM((rows, 128), F32),
            pltpu.VMEM((rows, 128), F32),
            pltpu.VMEM((cols // 128, rows, 128), F32),
            pltpu.VMEM((rows * cols // 128, 128), F32),
            pltpu.VMEM((2, entries, 128), F32),
            pltpu.VMEM(basis.shape, BF16),
            pltpu.VMEM((rows, cols), F32),
            pltpu.SemaphoreType.DMA((2,)),
        ],
        compiler_params=params(),
        cost_estimate=pl.CostEstimate(
            flops=10**9, bytes_accessed=6 << 20, transcendentals=0
        ),
        name="main",
    )(a, coef, *halo, basis, dest, sel)


def add_kernel(first, dest_ref, hi_ref, lo_ref, got_ref, out_ref):
    gather_rows(out_ref, dest_ref[...], hi_ref[...], lo_ref[...], first, got_ref)


def add_rows(first, count, dest, hi, lo, got):
    ncoef = got.shape[1]
    return pl.pallas_call(
        functools.partial(add_kernel, first),
        in_specs=[vmem()] * 4,
        out_specs=vmem(),
        out_shape=whole((count, ncoef)),
        compiler_params=params(),
        cost_estimate=pl.CostEstimate(
            flops=3 * 10**8, bytes_accessed=1 << 20, transcendentals=0
        ),
        name="add",
    )(dest, hi, lo, got)


def last_kernel(
    a_hbm, kap_hbm, elev_hbm, n_ref, s_ref, w_ref, e_ref, t_ref, b_ref, out_ref,
    a_ref, kap, elev, wt, et, sems,
):
    copies = [
        pltpu.make_async_copy(a_hbm, a_ref, sems.at[2]),
        pltpu.make_async_copy(kap_hbm, kap, sems.at[0]),
        pltpu.make_async_copy(elev_hbm, elev, sems.at[1]),
    ]
    for copy in copies:
        copy.start()
    wt[...] = column(w_ref)
    et[...] = column(e_ref)
    for copy in copies:
        copy.wait()

    def emit(r, x, new):
        out_ref[r : r + 8, :] = new

    def coef(r):
        e = elev[r : r + 8, :]
        return DT * kap[r : r + 8, :] / (1.0 + e * e)

    lane = lax.broadcasted_iota(I32, (1, a_ref.shape[1]), 1)
    beyond = []
    for k, (ref, own) in enumerate(((n_ref, t_ref), (s_ref, b_ref))):
        missing = own[0:1, :]
        missing += jnp.where(lane == 0, w_ref[:, 128 + k : 129 + k], 0.0)
        missing += jnp.where(lane == a_ref.shape[1] - 1, e_ref[:, 128 + k : 129 + k], 0.0)
        beyond.append(ref[1:2, :] + ref[2:3, :] * missing)
    stencil(a_ref, coef, *beyond, wt, et, emit)


def last(a, kappa, elev, halo, own):
    rows, cols = a.shape
    return pl.pallas_call(
        last_kernel,
        in_specs=[hbm()] * 3 + [vmem()] * 6,
        out_specs=vmem(),
        out_shape=whole((rows, cols)),
        scratch_shapes=[
            pltpu.VMEM((rows, cols), F32),
            pltpu.VMEM((rows, cols), F32),
            pltpu.VMEM((rows, cols), F32),
            pltpu.VMEM((rows, 128), F32),
            pltpu.VMEM((rows, 128), F32),
            pltpu.SemaphoreType.DMA((3,)),
        ],
        compiler_params=params(),
        cost_estimate=pl.CostEstimate(
            flops=10**7, bytes_accessed=2 << 20, transcendentals=0
        ),
        name="last",
    )(a, kappa, elev, *halo, *own)


def exchange(axis, low, high):
    count = lax.axis_size(axis)
    forward = [(i, i + 1) for i in range(count - 1)]
    backward = [(target, source) for source, target in forward]
    return [lax.ppermute(low, axis, forward), lax.ppermute(high, axis, backward)]


def swing(step):
    return (1 - (-2) ** (step + 1)) // 3


def partners(n_chip, step):
    pairs = []
    for z in range(n_chip):
        for core in range(2):
            sign = -1 if (z + core) % 2 else 1
            other = (z + sign * swing(step)) % n_chip
            pairs.append((2 * z + core, 2 * other + core))
    return pairs


def compute(
    adj_final, kappa, elev_early, elev_late, basis, basis_index, intersection_patch, owner_row
):
    n_row = lax.axis_size("row")
    total = owner_row.shape[1]
    place = lax.axis_index("row").astype(I32)
    top, bottom, left, right = edges(in_hbm(adj_final), in_hbm(kappa), in_hbm(elev_late))
    halo_row = exchange("row", bottom, top)
    halo = halo_row + exchange("col", right, left)
    dest, sel, coef = indices(
        place.reshape(1), intersection_patch[0], owner_row, basis_index[0], kappa, elev_late
    )
    mid, left, right, hi, lo, send = main(
        adj_final, coef, halo, in_hbm(basis[0, 0]), dest, sel, total
    )
    got = lax.ppermute(send, "row", [(i, i ^ 1) for i in range(n_row)])
    half = got.shape[0] // 2
    sent = add_rows(half, half, dest, hi, lo, got)
    part = add_rows(0, half, dest, hi, lo, got)
    halo_col = exchange("col", right, left)
    adj_start = last(mid, in_hbm(kappa), in_hbm(elev_early), halo_row + halo_col, (top, bottom))
    steps = (n_row // 2).bit_length() - 1
    for step in range(steps):
        got = lax.ppermute(sent, "row", partners(n_row // 2, step))
        if step == steps - 1:
            return (adj_start, (part + got)[None])
        half = part.shape[0] // 2
        sent = part[half:] + got[half:]
        part = part[:half] + got[:half]


def solution(mesh):
    return jax.shard_map(
        compute,
        mesh=mesh,
        in_specs=(
            P(("mem", "row"), "col"),
            P(("mem", "row"), "col"),
            P(("mem", "row"), "col"),
            P(("mem", "row"), "col"),
            P(("mem", "row"), "col", None, None, None),
            P(("mem", "row"), "col", None),
            P(("mem", "row"), "col", None),
            P(("mem", "col"), None),
        ),
        out_specs=(P(("mem", "row"), "col"), P(("mem", "col"), "row", None)),
        check_vma=False,
    )
```

```python
import functools

import jax
import jax.numpy as jnp
from jax import lax
from jax.experimental import pallas as pl
from jax.experimental.pallas import tpu as pltpu
from jax.sharding import PartitionSpec as P


BS = 32
DT = 0.2
F32 = jnp.float32
BF16 = jnp.bfloat16
I32 = jnp.int32
VLIM = 24 << 20


def whole(shape):
    return jax.ShapeDtypeStruct(shape, F32)


def vmem():
    return pl.BlockSpec(memory_space=pltpu.VMEM)


def hbm():
    return pl.BlockSpec(memory_space=pltpu.HBM)


def in_hbm(x):
    return pltpu.with_memory_space_constraint(x, pltpu.HBM)


def params(limit=VLIM):
    return pltpu.CompilerParams(vmem_limit_bytes=limit)


def paths(n_chip):
    steps = n_chip.bit_length() - 1
    spots = [0] * n_chip
    for path in range(n_chip):
        at = 0
        for step in range(steps):
            if (path >> (steps - 1 - step)) & 1:
                at += -swing(step) if at % 2 else swing(step)
        spots[at % n_chip] = path
    return spots


def edge_row(x, inner, kap, elev):
    lane = lax.broadcasted_iota(I32, x.shape, 1)
    last = x.shape[1] - 1
    east = jnp.where(lane == last, 0.0, pltpu.roll(x, last, 1))
    west = jnp.where(lane == 0, 0.0, pltpu.roll(x, 1, 1))
    coef = DT * kap / (1.0 + elev * elev)
    return x + coef * (inner + east + west - 4.0 * x), coef


def edges_kernel(
    n_row, n_col, place_ref, col_ref, top_ref, bot_ref, left_ref, right_ref, ktop_ref, kbot_ref, etop_ref, ebot_ref,
    t_ref, b_ref, l_ref, r_ref,
):
    top, bot = top_ref[...], bot_ref[...]
    partial, coef = edge_row(top, pltpu.roll(top, 7, 0), ktop_ref[...], etop_ref[...])
    inside = place_ref[0] > 0
    t_ref[0:1, :] = jnp.where(inside, top[0:1, :], 0.0)
    t_ref[1:2, :] = jnp.where(inside, partial[0:1, :], 0.0)
    t_ref[2:3, :] = jnp.where(inside, coef[0:1, :], 0.0)
    partial, coef = edge_row(bot, pltpu.roll(bot, 1, 0), kbot_ref[...], ebot_ref[...])
    inside = place_ref[0] < n_row - 1
    b_ref[0:1, :] = jnp.where(inside, bot[7:8, :], 0.0)
    b_ref[1:2, :] = jnp.where(inside, partial[7:8, :], 0.0)
    b_ref[2:3, :] = jnp.where(inside, coef[7:8, :], 0.0)
    l_ref[...] = jnp.where(col_ref[0] > 0, left_ref[...].T[0:1, :], 0.0)
    r_ref[...] = jnp.where(col_ref[0] < n_col - 1, right_ref[...].T[127:128, :], 0.0)


def edges(n_row, n_col, place, col, a, kappa, elev):
    rows, cols = a.shape
    first = pl.BlockSpec((8, cols), lambda i: (0, 0))
    final = pl.BlockSpec((8, cols), lambda i: (rows // 8 - 1, 0))
    return pl.pallas_call(
        functools.partial(edges_kernel, n_row, n_col),
        grid=(1,),
        in_specs=[
            pl.BlockSpec(memory_space=pltpu.SMEM),
            pl.BlockSpec(memory_space=pltpu.SMEM),
            first,
            final,
            pl.BlockSpec((rows, 128), lambda i: (0, 0)),
            pl.BlockSpec((rows, 128), lambda i: (0, cols // 128 - 1)),
            first,
            final,
            first,
            final,
        ],
        out_specs=[
            pl.BlockSpec((3, cols), lambda i: (0, 0)),
            pl.BlockSpec((3, cols), lambda i: (0, 0)),
            pl.BlockSpec((1, rows), lambda i: (0, 0)),
            pl.BlockSpec((1, rows), lambda i: (0, 0)),
        ],
        out_shape=[whole((3, cols)), whole((3, cols)), whole((1, rows)), whole((1, rows))],
        compiler_params=params(4 << 20),
        name="edges",
    )(place, col, a, a, a, a, kappa, kappa, elev, elev)


def index_kernel(
    place_ref, patch_ref, owner_ref, idx_ref, kap_ref, elev_ref, dest_ref, sel_ref, coef_ref
):
    for r in range(0, kap_ref.shape[0], 8):
        e = elev_ref[r : r + 8, :]
        coef_ref[r : r + 8, :] = DT * kap_ref[r : r + 8, :] / (1.0 + e * e)
    entries = patch_ref.shape[1]
    patches = owner_ref.shape[1]
    hot = lax.broadcasted_iota(I32, (patches, entries), 0) == patch_ref[...]
    hot = jnp.where(hot, 1.0, 0.0).astype(BF16)
    owner = owner_ref[...]
    row = lax.broadcasted_iota(I32, (16, patches), 0)
    parts = jnp.where(row == 0, owner >> 6, jnp.where(row == 1, owner & 63, 0))
    found = jnp.dot(parts.astype(F32).astype(BF16), hot, preferred_element_type=F32)
    high = found[0:1, :].astype(I32)
    core, chip = place_ref[0] & 1, place_ref[0] >> 1
    n_chip = patches // 128
    mirror = (chip + high) & 1
    away = (high >> 1) - chip
    away = jnp.where(mirror == 1, -away, away) & (n_chip - 1)
    low = found[1:2, :].astype(I32)
    spot = ((high & 1) ^ core) * n_chip
    for d, path in enumerate(paths(n_chip)):
        spot += jnp.where(away == d, path, 0)
    dest_ref[...] = spot * 64 + low
    nb = entries // 4
    lane = lax.broadcasted_iota(I32, (nb, entries), 1)
    block = lax.broadcasted_iota(I32, (nb, entries), 0)
    idx = jnp.broadcast_to(idx_ref[...], (nb, entries))
    for o in range(4):
        sel_ref[:, o : o + 1] = jnp.sum(
            jnp.where(lane == block * 4 + o, idx, 0), axis=1, keepdims=True
        )


def indices(place, patch, owner, idx, kappa, elev):
    entries = patch.shape[1]
    return pl.pallas_call(
        index_kernel,
        in_specs=[pl.BlockSpec(memory_space=pltpu.SMEM)] + [vmem()] * 5,
        out_specs=[vmem()] * 3,
        out_shape=[
            jax.ShapeDtypeStruct((1, entries), I32),
            jax.ShapeDtypeStruct((entries // 4, 4), I32),
            whole(kappa.shape),
        ],
        compiler_params=params(),
        name="indices",
    )(place, patch, owner, idx, kappa, elev)


def stencil(a_ref, coef_of, north, south, wt, et, emit):
    rows, cols = a_ref.shape
    lane = lax.broadcasted_iota(I32, (8, cols), 1)
    sub = lax.broadcasted_iota(I32, (8, cols), 0)
    for i in range(rows // 8):
        r = 8 * i
        x = a_ref[r : r + 8, :]
        if i == 0:
            up = jnp.where(sub == 0, north, pltpu.roll(x, 1, 0))
        else:
            up = a_ref[r - 1 : r + 7, :]
        if i == rows // 8 - 1:
            down = jnp.where(sub == 7, south, pltpu.roll(x, 7, 0))
        else:
            down = a_ref[r + 1 : r + 9, :]
        east = jnp.where(lane == cols - 1, et[r : r + 8, 0:1], pltpu.roll(x, cols - 1, 1))
        west = jnp.where(lane == 0, wt[r : r + 8, 0:1], pltpu.roll(x, 1, 1))
        lap = down + up + east + west - 4.0 * x
        emit(r, x, x + coef_of(r) * lap)


def column(ref):
    return jnp.broadcast_to(ref[:, 0:128], (128, 128)).T


def hot_rows(dest, start, count):
    entries = dest.shape[1]
    row = lax.broadcasted_iota(I32, (count, entries), 0) + start
    return jnp.where(row == dest, 1.0, 0.0).astype(BF16)


def gather_rows(out_ref, dest, hi, lo, first, got_ref=None):
    rows = out_ref.shape[0]
    step = 256
    for k in range(rows // step):
        hot = hot_rows(dest, first + k * step, step)
        total = jnp.dot(hot, hi, preferred_element_type=F32)
        total += jnp.dot(hot, lo, preferred_element_type=F32)
        if got_ref is not None:
            total += got_ref[first + k * step : first + (k + 1) * step, :]
        out_ref[k * step : (k + 1) * step, :] = total


def main_kernel(
    n_col, col_ref, a_ref, coef_ref, n_ref, s_ref, w_ref, e_ref, basis_ref, dest_ref, sel_ref,
    mid_hbm, l_ref, r_ref, hi_ref, lo_ref, send_ref,
    wt, et, g_ref, y_ref, c_ref, table, mid_ref, sems,
):
    rows, cols = a_ref.shape
    copy = pltpu.make_async_copy(basis_ref, table, sems.at[0])
    copy.start()
    wt[...] = column(w_ref)
    et[...] = column(e_ref)

    def emit(r, x, mid):
        mid_ref[r : r + 8, :] = mid
        g = DT * (x + mid)
        for k in range(cols // 128):
            g_ref[k, r : r + 8, :] = g[:, k * 128 : (k + 1) * 128]

    north, south = n_ref[0:1, :], s_ref[0:1, :]
    stencil(a_ref, lambda r: coef_ref[r : r + 8, :], north, south, wt, et, emit)
    stored = pltpu.make_async_copy(mid_ref, mid_hbm, sems.at[1])
    stored.start()
    nb = rows * cols // (BS * BS)
    chunk = lax.broadcasted_iota(I32, (8, 128), 1) // BS
    for br in range(rows // BS):
        for bh in range(cols // 128):
            v = [
                g_ref[bh, pl.ds(br * BS + rl, 8, stride=4), :]
                for rl in range(4)
            ]
            for bl in range(4):
                out = v[bl]
                for rl in range(4):
                    if rl != bl:
                        moved = pltpu.roll(v[rl], ((rl - bl) * BS) % 128, 1)
                        out = jnp.where(chunk == rl, moved, out)
                b = br * (cols // BS) + bh * 4 + bl
                y_ref[pl.ds(b, 8, stride=nb), :] = out
    lhs = jnp.concatenate(
        [y_ref[rh * nb : (rh + 1) * nb, :].astype(BF16) for rh in range(8)], axis=1
    )
    copy.wait()
    products = [
        jnp.dot(lhs, table[q], preferred_element_type=F32)
        for q in range(basis_ref.shape[0])
    ]
    for o in range(4):
        sel = sel_ref[:, o : o + 1]
        out = jnp.zeros_like(products[0])
        for q, product in enumerate(products):
            out = jnp.where(sel == q, product, out)
        for h in range(2):
            c_ref[h, pl.ds(o, nb, stride=4), :] = out[:, h * 128 : (h + 1) * 128]
    contrib = jnp.concatenate([c_ref[0], c_ref[1]], axis=1)
    hi = contrib.astype(BF16)
    lo = (contrib - hi.astype(F32)).astype(BF16)
    hi_ref[...] = hi
    lo_ref[...] = lo
    gather_rows(send_ref, dest_ref[...], hi, lo, send_ref.shape[0])
    lane = lax.broadcasted_iota(I32, (1, 128), 1)
    column_of = {0: mid_ref[:, 0:128].T[0:1, :]}
    column_of[cols - 1] = mid_ref[:, cols - 128 : cols].T[127:128, :]
    for out, k in ((l_ref, 0), (r_ref, cols - 1)):
        inside = (col_ref[0] > 0) if k == 0 else (col_ref[0] < n_col - 1)
        corner = jnp.where(lane == 1, south[:, k : k + 1], 0.0)
        corner = jnp.where(lane == 0, north[:, k : k + 1], corner)
        out[:, 0:128] = jnp.where(inside, column_of[k], 0.0)
        out[:, 128:256] = jnp.where(inside, corner, 0.0)
    stored.wait()


def main(n_col, col, a, coef, halo, basis, dest, sel, total):
    rows, cols = a.shape
    entries = dest.shape[1]
    ncoef = basis.shape[-1]
    return pl.pallas_call(
        functools.partial(main_kernel, n_col),
        in_specs=[pl.BlockSpec(memory_space=pltpu.SMEM)] + [vmem()] * 6 + [hbm()] + [vmem()] * 2,
        out_specs=[hbm()] + [vmem()] * 5,
        out_shape=[
            whole((rows, cols)),
            whole((1, 2 * rows)),
            whole((1, 2 * rows)),
            jax.ShapeDtypeStruct((entries, ncoef), BF16),
            jax.ShapeDtypeStruct((entries, ncoef), BF16),
            whole((total // 2, ncoef)),
        ],
        scratch_shapes=[
            pltpu.VMEM((rows, 128), F32),
            pltpu.VMEM((rows, 128), F32),
            pltpu.VMEM((cols // 128, rows, 128), F32),
            pltpu.VMEM((rows * cols // 128, 128), F32),
            pltpu.VMEM((2, entries, 128), F32),
            pltpu.VMEM(basis.shape, BF16),
            pltpu.VMEM((rows, cols), F32),
            pltpu.SemaphoreType.DMA((2,)),
        ],
        compiler_params=params(),
        cost_estimate=pl.CostEstimate(
            flops=10**9, bytes_accessed=6 << 20, transcendentals=0
        ),
        name="main",
    )(col, a, coef, *halo, basis, dest, sel)


def add_kernel(first, dest_ref, hi_ref, lo_ref, got_ref, out_ref):
    gather_rows(out_ref, dest_ref[...], hi_ref[...], lo_ref[...], first, got_ref)


def add_rows(first, count, dest, hi, lo, got):
    ncoef = got.shape[1]
    return pl.pallas_call(
        functools.partial(add_kernel, first),
        in_specs=[vmem()] * 4,
        out_specs=vmem(),
        out_shape=whole((count, ncoef)),
        compiler_params=params(),
        cost_estimate=pl.CostEstimate(
            flops=3 * 10**8, bytes_accessed=1 << 20, transcendentals=0
        ),
        name="add",
    )(dest, hi, lo, got)


def last_kernel(
    a_hbm, kap_hbm, elev_hbm, n_ref, s_ref, w_ref, e_ref, t_ref, b_ref, out_ref,
    a_ref, kap, elev, wt, et, sems,
):
    copies = [
        pltpu.make_async_copy(a_hbm, a_ref, sems.at[2]),
        pltpu.make_async_copy(kap_hbm, kap, sems.at[0]),
        pltpu.make_async_copy(elev_hbm, elev, sems.at[1]),
    ]
    for copy in copies:
        copy.start()
    wt[...] = column(w_ref)
    et[...] = column(e_ref)
    for copy in copies:
        copy.wait()

    def emit(r, x, new):
        out_ref[r : r + 8, :] = new

    def coef(r):
        e = elev[r : r + 8, :]
        return DT * kap[r : r + 8, :] / (1.0 + e * e)

    lane = lax.broadcasted_iota(I32, (1, a_ref.shape[1]), 1)
    beyond = []
    for k, (ref, own) in enumerate(((n_ref, t_ref), (s_ref, b_ref))):
        missing = own[0:1, :]
        missing += jnp.where(lane == 0, w_ref[:, 128 + k : 129 + k], 0.0)
        missing += jnp.where(lane == a_ref.shape[1] - 1, e_ref[:, 128 + k : 129 + k], 0.0)
        beyond.append(ref[1:2, :] + ref[2:3, :] * missing)
    stencil(a_ref, coef, *beyond, wt, et, emit)


def last(a, kappa, elev, halo, own):
    rows, cols = a.shape
    return pl.pallas_call(
        last_kernel,
        in_specs=[hbm()] * 3 + [vmem()] * 6,
        out_specs=vmem(),
        out_shape=whole((rows, cols)),
        scratch_shapes=[
            pltpu.VMEM((rows, cols), F32),
            pltpu.VMEM((rows, cols), F32),
            pltpu.VMEM((rows, cols), F32),
            pltpu.VMEM((rows, 128), F32),
            pltpu.VMEM((rows, 128), F32),
            pltpu.SemaphoreType.DMA((3,)),
        ],
        compiler_params=params(),
        cost_estimate=pl.CostEstimate(
            flops=10**7, bytes_accessed=2 << 20, transcendentals=0
        ),
        name="last",
    )(a, kappa, elev, *halo, *own)


def exchange(axis, low, high):
    count = lax.axis_size(axis)
    forward = [(i, (i + 1) % count) for i in range(count)]
    backward = [(target, source) for source, target in forward]
    return [lax.ppermute(low, axis, forward), lax.ppermute(high, axis, backward)]


def swing(step):
    return (1 - (-2) ** (step + 1)) // 3


def partners(n_chip, step):
    pairs = []
    for z in range(n_chip):
        for core in range(2):
            sign = -1 if (z + core) % 2 else 1
            other = (z + sign * swing(step)) % n_chip
            pairs.append((2 * z + core, 2 * other + core))
    return pairs


def compute(
    adj_final, kappa, elev_early, elev_late, basis, basis_index, intersection_patch, owner_row
):
    n_row = lax.axis_size("row")
    total = owner_row.shape[1]
    n_col = lax.axis_size("col")
    place = lax.axis_index("row").astype(I32)
    col = lax.axis_index("col").astype(I32).reshape(1)
    top, bottom, left, right = edges(
        n_row, n_col, place.reshape(1), col, in_hbm(adj_final), in_hbm(kappa),
        in_hbm(elev_late),
    )
    halo_col = exchange("col", right, left)
    halo_row = exchange("row", bottom, top)
    halo = halo_row + halo_col
    dest, sel, coef = indices(
        place.reshape(1), intersection_patch[0], owner_row, basis_index[0], kappa, elev_late
    )
    mid, left, right, hi, lo, send = main(
        n_col, col, adj_final, coef, halo, in_hbm(basis[0, 0]), dest, sel, total
    )
    got = lax.ppermute(send, "row", [(i, i ^ 1) for i in range(n_row)])
    half = got.shape[0] // 2
    sent = add_rows(half, half, dest, hi, lo, got)
    part = add_rows(0, half, dest, hi, lo, got)
    halo_col = exchange("col", right, left)
    adj_start = last(mid, in_hbm(kappa), in_hbm(elev_early), halo_row + halo_col, (top, bottom))
    steps = (n_row // 2).bit_length() - 1
    for step in range(steps):
        got = lax.ppermute(sent, "row", partners(n_row // 2, step))
        if step == steps - 1:
            return (adj_start, (part + got)[None])
        half = part.shape[0] // 2
        sent = part[half:] + got[half:]
        part = part[:half] + got[:half]


def solution(mesh):
    return jax.shard_map(
        compute,
        mesh=mesh,
        in_specs=(
            P(("mem", "row"), "col"),
            P(("mem", "row"), "col"),
            P(("mem", "row"), "col"),
            P(("mem", "row"), "col"),
            P(("mem", "row"), "col", None, None, None),
            P(("mem", "row"), "col", None),
            P(("mem", "row"), "col", None),
            P(("mem", "col"), None),
        ),
        out_specs=(P(("mem", "row"), "col"), P(("mem", "col"), "row", None)),
        check_vma=False,
    )
```

```python
import functools

import jax
import jax.numpy as jnp
from jax import lax
from jax.experimental import pallas as pl
from jax.experimental.pallas import tpu as pltpu
from jax.sharding import PartitionSpec as P


BS = 32
DT = 0.2
F32 = jnp.float32
BF16 = jnp.bfloat16
I32 = jnp.int32
VLIM = 24 << 20


def whole(shape):
    return jax.ShapeDtypeStruct(shape, F32)


def vmem():
    return pl.BlockSpec(memory_space=pltpu.VMEM)


def hbm():
    return pl.BlockSpec(memory_space=pltpu.HBM)


def in_hbm(x):
    return pltpu.with_memory_space_constraint(x, pltpu.HBM)


def params(limit=VLIM):
    return pltpu.CompilerParams(vmem_limit_bytes=limit)


def paths(n_chip):
    steps = n_chip.bit_length() - 1
    spots = [0] * n_chip
    for path in range(n_chip):
        at = 0
        for step in range(steps):
            if (path >> (steps - 1 - step)) & 1:
                at += -swing(step) if at % 2 else swing(step)
        spots[at % n_chip] = path
    return spots


def edge_row(x, inner, kap, elev):
    lane = lax.broadcasted_iota(I32, x.shape, 1)
    last = x.shape[1] - 1
    east = jnp.where(lane == last, 0.0, pltpu.roll(x, last, 1))
    west = jnp.where(lane == 0, 0.0, pltpu.roll(x, 1, 1))
    coef = DT * kap / (1.0 + elev * elev)
    return x + coef * (inner + east + west - 4.0 * x), coef


def edges_kernel(
    n_row, n_col, place_ref, col_ref, top_ref, bot_ref, left_ref, right_ref, ktop_ref, kbot_ref, etop_ref, ebot_ref,
    t_ref, b_ref, l_ref, r_ref,
):
    top, bot = top_ref[...], bot_ref[...]
    partial, coef = edge_row(top, pltpu.roll(top, 7, 0), ktop_ref[...], etop_ref[...])
    inside = place_ref[0] > 0
    t_ref[0:1, :] = jnp.where(inside, top[0:1, :], 0.0)
    t_ref[1:2, :] = jnp.where(inside, partial[0:1, :], 0.0)
    t_ref[2:3, :] = jnp.where(inside, coef[0:1, :], 0.0)
    partial, coef = edge_row(bot, pltpu.roll(bot, 1, 0), kbot_ref[...], ebot_ref[...])
    inside = place_ref[0] < n_row - 1
    b_ref[0:1, :] = jnp.where(inside, bot[7:8, :], 0.0)
    b_ref[1:2, :] = jnp.where(inside, partial[7:8, :], 0.0)
    b_ref[2:3, :] = jnp.where(inside, coef[7:8, :], 0.0)
    l_ref[...] = jnp.where(col_ref[0] > 0, left_ref[...].T[0:1, :], 0.0)
    r_ref[...] = jnp.where(col_ref[0] < n_col - 1, right_ref[...].T[127:128, :], 0.0)


def edges(n_row, n_col, place, col, a, kappa, elev):
    rows, cols = a.shape
    first = pl.BlockSpec((8, cols), lambda i: (0, 0))
    final = pl.BlockSpec((8, cols), lambda i: (rows // 8 - 1, 0))
    return pl.pallas_call(
        functools.partial(edges_kernel, n_row, n_col),
        grid=(1,),
        in_specs=[
            pl.BlockSpec(memory_space=pltpu.SMEM),
            pl.BlockSpec(memory_space=pltpu.SMEM),
            first,
            final,
            pl.BlockSpec((rows, 128), lambda i: (0, 0)),
            pl.BlockSpec((rows, 128), lambda i: (0, cols // 128 - 1)),
            first,
            final,
            first,
            final,
        ],
        out_specs=[
            pl.BlockSpec((3, cols), lambda i: (0, 0)),
            pl.BlockSpec((3, cols), lambda i: (0, 0)),
            pl.BlockSpec((1, rows), lambda i: (0, 0)),
            pl.BlockSpec((1, rows), lambda i: (0, 0)),
        ],
        out_shape=[whole((3, cols)), whole((3, cols)), whole((1, rows)), whole((1, rows))],
        compiler_params=params(4 << 20),
        name="edges",
    )(place, col, a, a, a, a, kappa, kappa, elev, elev)


def index_kernel(
    place_ref, patch_ref, owner_ref, idx_ref, kap_hbm, elev_hbm, dest_ref, sel_ref, coef_ref,
    kap_ref, elev_ref, sems,
):
    copies = [
        pltpu.make_async_copy(kap_hbm, kap_ref, sems.at[0]),
        pltpu.make_async_copy(elev_hbm, elev_ref, sems.at[1]),
    ]
    for copy in copies:
        copy.start()
    entries = patch_ref.shape[1]
    patches = owner_ref.shape[1]
    hot = lax.broadcasted_iota(I32, (patches, entries), 0) == patch_ref[...]
    hot = jnp.where(hot, 1.0, 0.0).astype(BF16)
    owner = owner_ref[...]
    row = lax.broadcasted_iota(I32, (16, patches), 0)
    parts = jnp.where(row == 0, owner >> 6, jnp.where(row == 1, owner & 63, 0))
    found = jnp.dot(parts.astype(F32).astype(BF16), hot, preferred_element_type=F32)
    high = found[0:1, :].astype(I32)
    core, chip = place_ref[0] & 1, place_ref[0] >> 1
    n_chip = patches // 128
    mirror = (chip + high) & 1
    away = (high >> 1) - chip
    away = jnp.where(mirror == 1, -away, away) & (n_chip - 1)
    low = found[1:2, :].astype(I32)
    spot = ((high & 1) ^ core) * n_chip
    for d, path in enumerate(paths(n_chip)):
        spot += jnp.where(away == d, path, 0)
    dest_ref[...] = spot * 64 + low
    nb = entries // 4
    lane = lax.broadcasted_iota(I32, (nb, entries), 1)
    block = lax.broadcasted_iota(I32, (nb, entries), 0)
    idx = jnp.broadcast_to(idx_ref[...], (nb, entries))
    for o in range(4):
        sel_ref[:, o : o + 1] = jnp.sum(
            jnp.where(lane == block * 4 + o, idx, 0), axis=1, keepdims=True
        )
    for copy in copies:
        copy.wait()
    for r in range(0, kap_ref.shape[0], 8):
        e = elev_ref[r : r + 8, :]
        coef_ref[r : r + 8, :] = DT * kap_ref[r : r + 8, :] / (1.0 + e * e)


def indices(place, patch, owner, idx, kappa, elev):
    entries = patch.shape[1]
    return pl.pallas_call(
        index_kernel,
        in_specs=[pl.BlockSpec(memory_space=pltpu.SMEM)] + [vmem()] * 3 + [hbm()] * 2,
        out_specs=[vmem()] * 3,
        out_shape=[
            jax.ShapeDtypeStruct((1, entries), I32),
            jax.ShapeDtypeStruct((entries // 4, 4), I32),
            whole(kappa.shape),
        ],
        scratch_shapes=[
            pltpu.VMEM(kappa.shape, F32),
            pltpu.VMEM(kappa.shape, F32),
            pltpu.SemaphoreType.DMA((2,)),
        ],
        compiler_params=params(),
        name="indices",
    )(place, patch, owner, idx, kappa, elev)


def stencil(a_ref, coef_of, north, south, wt, et, emit):
    rows, cols = a_ref.shape
    lane = lax.broadcasted_iota(I32, (8, cols), 1)
    sub = lax.broadcasted_iota(I32, (8, cols), 0)
    for i in range(rows // 8):
        r = 8 * i
        x = a_ref[r : r + 8, :]
        if i == 0:
            up = jnp.where(sub == 0, north, pltpu.roll(x, 1, 0))
        else:
            up = a_ref[r - 1 : r + 7, :]
        if i == rows // 8 - 1:
            down = jnp.where(sub == 7, south, pltpu.roll(x, 7, 0))
        else:
            down = a_ref[r + 1 : r + 9, :]
        east = jnp.where(lane == cols - 1, et[r : r + 8, 0:1], pltpu.roll(x, cols - 1, 1))
        west = jnp.where(lane == 0, wt[r : r + 8, 0:1], pltpu.roll(x, 1, 1))
        lap = down + up + east + west - 4.0 * x
        emit(r, x, x + coef_of(r) * lap)


def column(ref):
    return jnp.broadcast_to(ref[:, 0:128], (128, 128)).T


def hot_rows(dest, start, count):
    entries = dest.shape[1]
    row = lax.broadcasted_iota(I32, (count, entries), 0) + start
    return jnp.where(row == dest, 1.0, 0.0).astype(BF16)


def gather_rows(out_ref, dest, hi, lo, first, got_ref=None):
    rows = out_ref.shape[0]
    step = 256
    for k in range(rows // step):
        hot = hot_rows(dest, first + k * step, step)
        total = jnp.dot(hot, hi, preferred_element_type=F32)
        total += jnp.dot(hot, lo, preferred_element_type=F32)
        if got_ref is not None:
            total += got_ref[first + k * step : first + (k + 1) * step, :]
        out_ref[k * step : (k + 1) * step, :] = total


def main_kernel(
    n_col, col_ref, a_ref, coef_ref, n_ref, s_ref, w_ref, e_ref, basis_ref, dest_ref, sel_ref,
    mid_hbm, l_ref, r_ref, hi_ref, lo_ref, send_ref,
    wt, et, g_ref, y_ref, c_ref, mid_ref, sem,
):
    rows, cols = a_ref.shape
    wt[...] = column(w_ref)
    et[...] = column(e_ref)

    def emit(r, x, mid):
        mid_ref[r : r + 8, :] = mid
        g = DT * (x + mid)
        for k in range(cols // 128):
            g_ref[k, r : r + 8, :] = g[:, k * 128 : (k + 1) * 128]

    north, south = n_ref[0:1, :], s_ref[0:1, :]
    stencil(a_ref, lambda r: coef_ref[r : r + 8, :], north, south, wt, et, emit)
    stored = pltpu.make_async_copy(mid_ref, mid_hbm, sem)
    stored.start()
    nb = rows * cols // (BS * BS)
    chunk = lax.broadcasted_iota(I32, (8, 128), 1) // BS
    for br in range(rows // BS):
        for bh in range(cols // 128):
            v = [
                g_ref[bh, pl.ds(br * BS + rl, 8, stride=4), :]
                for rl in range(4)
            ]
            for bl in range(4):
                out = v[bl]
                for rl in range(4):
                    if rl != bl:
                        moved = pltpu.roll(v[rl], ((rl - bl) * BS) % 128, 1)
                        out = jnp.where(chunk == rl, moved, out)
                b = br * (cols // BS) + bh * 4 + bl
                y_ref[pl.ds(b, 8, stride=nb), :] = out
    lhs = jnp.concatenate(
        [y_ref[rh * nb : (rh + 1) * nb, :].astype(BF16) for rh in range(8)], axis=1
    )
    products = [
        jnp.dot(lhs, basis_ref[q], preferred_element_type=F32)
        for q in range(basis_ref.shape[0])
    ]
    for o in range(4):
        sel = sel_ref[:, o : o + 1]
        out = jnp.zeros_like(products[0])
        for q, product in enumerate(products):
            out = jnp.where(sel == q, product, out)
        for h in range(2):
            c_ref[h, pl.ds(o, nb, stride=4), :] = out[:, h * 128 : (h + 1) * 128]
    contrib = jnp.concatenate([c_ref[0], c_ref[1]], axis=1)
    hi = contrib.astype(BF16)
    lo = (contrib - hi.astype(F32)).astype(BF16)
    hi_ref[...] = hi
    lo_ref[...] = lo
    gather_rows(send_ref, dest_ref[...], hi, lo, send_ref.shape[0])
    lane = lax.broadcasted_iota(I32, (1, 128), 1)
    column_of = {0: mid_ref[:, 0:128].T[0:1, :]}
    column_of[cols - 1] = mid_ref[:, cols - 128 : cols].T[127:128, :]
    for out, k in ((l_ref, 0), (r_ref, cols - 1)):
        inside = (col_ref[0] > 0) if k == 0 else (col_ref[0] < n_col - 1)
        corner = jnp.where(lane == 1, south[:, k : k + 1], 0.0)
        corner = jnp.where(lane == 0, north[:, k : k + 1], corner)
        out[:, 0:128] = jnp.where(inside, column_of[k], 0.0)
        out[:, 128:256] = jnp.where(inside, corner, 0.0)
    stored.wait()


def main(n_col, col, a, coef, halo, basis, dest, sel, total):
    rows, cols = a.shape
    entries = dest.shape[1]
    ncoef = basis.shape[-1]
    return pl.pallas_call(
        functools.partial(main_kernel, n_col),
        in_specs=[pl.BlockSpec(memory_space=pltpu.SMEM)] + [vmem()] * 9,
        out_specs=[hbm()] + [vmem()] * 5,
        out_shape=[
            whole((rows, cols)),
            whole((1, 2 * rows)),
            whole((1, 2 * rows)),
            jax.ShapeDtypeStruct((entries, ncoef), BF16),
            jax.ShapeDtypeStruct((entries, ncoef), BF16),
            whole((total // 2, ncoef)),
        ],
        scratch_shapes=[
            pltpu.VMEM((rows, 128), F32),
            pltpu.VMEM((rows, 128), F32),
            pltpu.VMEM((cols // 128, rows, 128), F32),
            pltpu.VMEM((rows * cols // 128, 128), F32),
            pltpu.VMEM((2, entries, 128), F32),
            pltpu.VMEM((rows, cols), F32),
            pltpu.SemaphoreType.DMA,
        ],
        compiler_params=params(),
        cost_estimate=pl.CostEstimate(
            flops=10**9, bytes_accessed=6 << 20, transcendentals=0
        ),
        name="main",
    )(col, a, coef, *halo, basis, dest, sel)


def add_kernel(first, dest_ref, hi_ref, lo_ref, got_ref, out_ref):
    gather_rows(out_ref, dest_ref[...], hi_ref[...], lo_ref[...], first, got_ref)


def add_rows(first, count, dest, hi, lo, got):
    ncoef = got.shape[1]
    return pl.pallas_call(
        functools.partial(add_kernel, first),
        in_specs=[vmem()] * 4,
        out_specs=vmem(),
        out_shape=whole((count, ncoef)),
        compiler_params=params(),
        cost_estimate=pl.CostEstimate(
            flops=3 * 10**8, bytes_accessed=1 << 20, transcendentals=0
        ),
        name="add",
    )(dest, hi, lo, got)


def last_kernel(
    a_hbm, kap_hbm, elev_hbm, n_ref, s_ref, w_ref, e_ref, t_ref, b_ref, out_ref,
    a_ref, kap, elev, wt, et, sems,
):
    copies = [
        pltpu.make_async_copy(a_hbm, a_ref, sems.at[2]),
        pltpu.make_async_copy(kap_hbm, kap, sems.at[0]),
        pltpu.make_async_copy(elev_hbm, elev, sems.at[1]),
    ]
    for copy in copies:
        copy.start()
    wt[...] = column(w_ref)
    et[...] = column(e_ref)
    for copy in copies:
        copy.wait()

    def emit(r, x, new):
        out_ref[r : r + 8, :] = new

    def coef(r):
        e = elev[r : r + 8, :]
        return DT * kap[r : r + 8, :] / (1.0 + e * e)

    lane = lax.broadcasted_iota(I32, (1, a_ref.shape[1]), 1)
    beyond = []
    for k, (ref, own) in enumerate(((n_ref, t_ref), (s_ref, b_ref))):
        missing = own[0:1, :]
        missing += jnp.where(lane == 0, w_ref[:, 128 + k : 129 + k], 0.0)
        missing += jnp.where(lane == a_ref.shape[1] - 1, e_ref[:, 128 + k : 129 + k], 0.0)
        beyond.append(ref[1:2, :] + ref[2:3, :] * missing)
    stencil(a_ref, coef, *beyond, wt, et, emit)


def last(a, kappa, elev, halo, own):
    rows, cols = a.shape
    return pl.pallas_call(
        last_kernel,
        in_specs=[hbm()] * 3 + [vmem()] * 6,
        out_specs=vmem(),
        out_shape=whole((rows, cols)),
        scratch_shapes=[
            pltpu.VMEM((rows, cols), F32),
            pltpu.VMEM((rows, cols), F32),
            pltpu.VMEM((rows, cols), F32),
            pltpu.VMEM((rows, 128), F32),
            pltpu.VMEM((rows, 128), F32),
            pltpu.SemaphoreType.DMA((3,)),
        ],
        compiler_params=params(),
        cost_estimate=pl.CostEstimate(
            flops=10**7, bytes_accessed=2 << 20, transcendentals=0
        ),
        name="last",
    )(a, kappa, elev, *halo, *own)


def exchange(axis, low, high):
    count = lax.axis_size(axis)
    forward = [(i, (i + 1) % count) for i in range(count)]
    backward = [(target, source) for source, target in forward]
    return [lax.ppermute(low, axis, forward), lax.ppermute(high, axis, backward)]


def swing(step):
    return (1 - (-2) ** (step + 1)) // 3


def partners(n_chip, step):
    pairs = []
    for z in range(n_chip):
        for core in range(2):
            sign = -1 if (z + core) % 2 else 1
            other = (z + sign * swing(step)) % n_chip
            pairs.append((2 * z + core, 2 * other + core))
    return pairs


def compute(
    adj_final, kappa, elev_early, elev_late, basis, basis_index, intersection_patch, owner_row
):
    n_row = lax.axis_size("row")
    total = owner_row.shape[1]
    n_col = lax.axis_size("col")
    place = lax.axis_index("row").astype(I32)
    col = lax.axis_index("col").astype(I32).reshape(1)
    top, bottom, left, right = edges(
        n_row, n_col, place.reshape(1), col, in_hbm(adj_final), in_hbm(kappa),
        in_hbm(elev_late),
    )
    halo_col = exchange("col", right, left)
    halo_row = exchange("row", bottom, top)
    halo = halo_row + halo_col
    dest, sel, coef = indices(
        place.reshape(1), intersection_patch[0], owner_row, basis_index[0],
        in_hbm(kappa), in_hbm(elev_late),
    )
    mid, left, right, hi, lo, send = main(
        n_col, col, adj_final, coef, halo, basis[0, 0], dest, sel, total
    )
    got = lax.ppermute(send, "row", [(i, i ^ 1) for i in range(n_row)])
    half = got.shape[0] // 2
    sent = add_rows(half, half, dest, hi, lo, got)
    part = add_rows(0, half, dest, hi, lo, got)
    halo_col = exchange("col", right, left)
    adj_start = last(mid, in_hbm(kappa), in_hbm(elev_early), halo_row + halo_col, (top, bottom))
    steps = (n_row // 2).bit_length() - 1
    for step in range(steps):
        got = lax.ppermute(sent, "row", partners(n_row // 2, step))
        if step == steps - 1:
            return (adj_start, (part + got)[None])
        half = part.shape[0] // 2
        sent = part[half:] + got[half:]
        part = part[:half] + got[:half]


def solution(mesh):
    return jax.shard_map(
        compute,
        mesh=mesh,
        in_specs=(
            P(("mem", "row"), "col"),
            P(("mem", "row"), "col"),
            P(("mem", "row"), "col"),
            P(("mem", "row"), "col"),
            P(("mem", "row"), "col", None, None, None),
            P(("mem", "row"), "col", None),
            P(("mem", "row"), "col", None),
            P(("mem", "col"), None),
        ),
        out_specs=(P(("mem", "row"), "col"), P(("mem", "col"), "row", None)),
        check_vma=False,
    )
```
